32 devices in a mesh: clips: 2 (over x), rows: 16 (over z, y, core).
Axes of the slice: x: 2, y: 2, z: 4, core: 2. Of those that a mesh axis runs over, the one named last changes fastest.
Arguments:
- state_start: bfloat16 [1024, 128, 128], P(('clips', 'rows')), parts along dimension 0, may hold values from -6 to 6
- features: bfloat16 [2, 1024, 128, 128], P(None, ('clips', 'rows')), parts along dimension 1, may hold values from -6 to 6
- row_moves: int32 [2, 2048], P(None, ('clips', 'rows')), parts along dimension 1, may hold values from -4 to 4, as said below
- col_moves: int32 [2, 2048], P(None, ('clips', 'rows')), parts along dimension 1, may hold values from -4 to 4
- merging_weight: bfloat16 [3, 3, 256, 128], replicated, may hold values from -0.125 to 0.125
- first_weight: bfloat16 [3, 3, 128, 128], replicated, may hold values from -0.1875 to 0.1875
- second_weight: bfloat16 [3, 3, 128, 128], replicated, may hold values from -0.1875 to 0.1875
Outputs:
- states: bfloat16 [2, 1024, 128, 128], P(None, ('clips', 'rows')), parts along dimension 1
The draws below stay inside these ranges and needn't reach their ends.
There are 2 independent parts, one for each index of `clips`. The reference program is written for one: setup_inputs(seed, part) draws one part's arguments, and reference() takes and returns one part's arrays. A program takes and returns all parts, laid end to end along the dimension named above; an argument that names none is the same for every part. Nothing has to cross between parts.
Inputs may be any that keep to these rules, and one draw needn't show every extreme that they name: `row_moves`: every source block lies on the destination block's own device or on the device just above or below it; in each frame, among the 64 destination blocks of one device at most 32 take their source from the device above and at most 32 from the device below, and some device takes exactly 32 from the device above and some device exactly 32 from the one below.
All inputs are finite; a program needn't handle non-finite values.
Results may differ from the reference program's by a relative error of at most 0.009.
Values may be sent and summed in bfloat16 or wider, within the bound.
No kernel may reach another device: no remote copies, remote signals or barrier semaphores. Data moves between devices by JAX's collectives and lax.ppermute only.
A program may use at most 64 MiB of HBM per device.

```python
import jax
import jax.numpy as jnp

C = 128
FRAMES = 2
MOVE = 4
ROWS_DEV = 32
W = 128
H = 512
BLOCKS = 1024
N_ROWS = 16


def draw_row_moves(key, part):
    band = ROWS_DEV // 8
    across = W // 8
    key_speed, key_sign, key_force, key_cols, key_jitter = jax.random.split(key, 5)
    level = jax.random.randint(key_speed, (FRAMES, N_ROWS), 0, 8)
    speed = jnp.where(level < 2, MOVE, level % 2)
    sign = jnp.where(jax.random.randint(key_sign, (FRAMES, N_ROWS), 0, 2) == 0, -1, 1)
    forced = jax.random.randint(key_force, (FRAMES, 1), 1, N_ROWS - 2)
    device = jnp.arange(N_ROWS)[None, :]
    speed = jnp.where((device == forced) | (device == forced + 1), MOVE, speed)
    sign = jnp.where(device == forced, -1, jnp.where(device == forced + 1, 1, sign))
    col_keys = jax.random.split(key_cols, FRAMES * N_ROWS)
    ranking = jax.vmap(lambda one_key: jax.random.permutation(one_key, across))(col_keys)
    ranking = ranking.reshape(FRAMES, N_ROWS, 1, across)
    moving = ranking < across // 2
    row_in = jnp.arange(band)[None, None, :, None]
    jitter = jax.random.randint(key_jitter, (FRAMES, N_ROWS, band, across), -1, 2)
    still = jnp.clip(row_in + jitter, 0, band - 1) - row_in
    fast = (sign * speed)[:, :, None, None]
    moves = jnp.where(moving, fast, still)
    return moves.reshape(FRAMES, BLOCKS).astype(jnp.int32)


def touch_ends(drawn, own_key, low, high):
    longest = drawn.shape.index(max(drawn.shape))
    spots = []
    for shift in (0, 1):
        where = [jax.random.randint(jax.random.fold_in(own_key, axis), (), 0, length) for axis, length in enumerate(drawn.shape)]
        where[longest] = (where[longest] + shift) % drawn.shape[longest]
        spots.append(tuple(where))
    return drawn.at[spots[0]].set(low).at[spots[1]].set(high)


def block_levels(key, extent, cuts, low, largest):
    def one(dim, shards_of):
        draws = jax.random.uniform(jax.random.fold_in(jax.random.fold_in(key, 6), dim), (shards_of,), jnp.float32, low / len(cuts), largest / len(cuts))
        return jnp.repeat(jnp.exp(draws), extent[dim] // shards_of).reshape((-1,) + (1,) * (len(extent) - dim - 1))

    loudness = one(*cuts[0])
    for cut in cuts[1:]:
        loudness = loudness * one(*cut)
    return loudness


def bell_draw(own_key, dims, deviation, limit, cuts=(), kind=jnp.bfloat16):
    result = deviation * jax.random.normal(own_key, dims, jnp.float32)
    if cuts:
        result = result * block_levels(own_key, dims, cuts, -0.22, 0.18)
    return jnp.clip(result, -limit, limit).astype(kind)


def setup_inputs(seed: int = 0, part: int = 0) -> dict:
    arg_keys = jax.random.split(jax.random.key(seed), 8)
    part_splits = jax.random.split(jax.random.fold_in(arg_keys[7], part), 8)
    return {
        "state_start": bell_draw(part_splits[0], (H, W, C), 1.0, 6.0, ((0, 16),)),
        "features": bell_draw(part_splits[1], (FRAMES, H, W, C), 1.0, 6.0, ((1, 16),)),
        "row_moves": draw_row_moves(jax.random.fold_in(jax.random.fold_in(arg_keys[7], part), 71), part),
        "col_moves": touch_ends(jax.random.randint(part_splits[3], (FRAMES, BLOCKS), -4, 5), jax.random.fold_in(part_splits[3], 1), -4, 4).astype(jnp.int32),
        "merging_weight": bell_draw(arg_keys[4], (3, 3, 2 * C, C), (9 * 2 * C) ** -0.5, 0.125),
        "first_weight": bell_draw(arg_keys[5], (3, 3, C, C), (9 * C) ** -0.5, 0.1875),
        "second_weight": bell_draw(arg_keys[6], (3, 3, C, C), (9 * C) ** -0.5, 0.1875),
    }


def convolve(padded, weight):
    out_rows = padded.shape[0] - 2
    col_count = padded.shape[1]
    in_chan = padded.shape[2]
    widened = jnp.pad(padded, ((0, 0), (1, 1), (0, 0)))
    shifted = jnp.concatenate([widened[:, 0:col_count], widened[:, 1:col_count + 1], widened[:, 2:col_count + 2]], axis=-1)
    summed = jnp.zeros((out_rows * col_count, weight.shape[3]), jnp.float32)
    for row_step in range(3):
        window = shifted[row_step:row_step + out_rows].reshape(out_rows * col_count, 3 * in_chan)
        taps = weight[row_step].reshape(3 * in_chan, weight.shape[3])
        summed = summed + jnp.dot(window, taps, preferred_element_type=jnp.float32)
    return summed.reshape(out_rows, col_count, weight.shape[3])


def pad_rows(field):
    return jnp.pad(field, ((1, 1), (0, 0), (0, 0)))


def fetch(previous, moves_down, moves_across):
    row_count, col_count, chan_count = previous.shape
    band_total = row_count // 8
    across = col_count // 8
    block_ids = jnp.arange(band_total * across).astype(jnp.int32)
    source_row = jnp.clip(block_ids // across + moves_down, 0, band_total - 1).astype(jnp.int32)
    source_col = jnp.clip(block_ids % across + moves_across, 0, across - 1).astype(jnp.int32)
    blocked = previous.reshape(band_total, 8, across, 8, chan_count)
    picked = blocked[source_row, :, source_col]
    picked = picked.reshape(band_total, across, 8, 8, chan_count)
    return picked.transpose(0, 2, 1, 3, 4).reshape(row_count, col_count, chan_count)


def reference(state_start, features, row_moves, col_moves, merging_weight, first_weight, second_weight):
    previous = state_start
    results = []
    for frame in range(FRAMES):
        warped = fetch(previous, row_moves[frame], col_moves[frame])
        joined = jnp.concatenate([features[frame], warped], axis=-1)
        raw = convolve(pad_rows(joined), merging_weight)
        merging = jnp.maximum(raw, 0.1 * raw).astype(jnp.bfloat16)
        middle = jnp.maximum(convolve(pad_rows(merging), first_weight), 0.0).astype(jnp.bfloat16)
        updated = (merging.astype(jnp.float32) + convolve(pad_rows(middle), second_weight)).astype(jnp.bfloat16)
        results.append(updated)
        previous = updated
    return jnp.stack(results)
```

```python
import functools

import jax
import jax.numpy as jnp
from jax import lax
from jax.experimental import pallas as pl
from jax.experimental.pallas import tpu as pltpu
from jax.sharding import PartitionSpec as P

BLK = 8
HALO = 3
VMEM = pl.BlockSpec(memory_space=pltpu.VMEM)
SMEM = pl.BlockSpec(memory_space=pltpu.SMEM)
ANY = pl.BlockSpec(memory_space=pl.ANY)
BF16 = jnp.bfloat16
F32 = jnp.float32


def shape_of(shape, dtype=BF16):
    return jax.ShapeDtypeStruct(shape, dtype)


def swap(x, axis, first):
    size = lax.axis_size(axis)
    pairs = []
    for i in range(first, size - 1, 2):
        pairs += [(i, i + 1), (i + 1, i)]
    return lax.ppermute(x, axis, pairs)


def swap_both(for_even, for_odd):
    far = swap(for_odd, "rows", 1)
    near = swap(for_even, "rows", 0)
    return near, far


def tables_kernel(band, across, slots, place_ref, row_ref, col_ref, feat_ref,
                  table_ref, near_ref, far_ref, near_edge, far_edge, sem):
    frames, blocks = row_ref.shape
    rows = feat_ref.shape[1]
    mine = place_ref[0]
    total = place_ref[1]
    odd = lax.rem(mine, 2)
    near_start = jnp.where(odd == 0, rows - HALO, 0)
    far_start = jnp.where(odd == 0, 0, rows - HALO)
    copies = [
        pltpu.make_async_copy(feat_ref.at[:, pl.ds(near_start, HALO)], near_edge, sem.at[0]),
        pltpu.make_async_copy(feat_ref.at[:, pl.ds(far_start, HALO)], far_edge, sem.at[1]),
    ]
    for copy in copies:
        copy.start()
    for frame in range(frames):
        def clear(slot, _):
            near_ref[frame, slot] = 0
            far_ref[frame, slot] = 0
            return 0

        lax.fori_loop(0, near_ref.shape[1], clear, 0)

        def visit(block, counts):
            near_count, far_count = counts
            row = lax.div(block, across)
            col = lax.rem(block, across)
            source = mine * band + row + row_ref[frame, block]
            source = jnp.clip(source, 0, total - 1) - mine * band
            column = jnp.clip(col + col_ref[frame, block], 0, across - 1)
            above = (source < 0).astype(jnp.int32)
            below = (source >= band).astype(jnp.int32)
            local = (source + (above - below) * band) * across + column
            is_near = jnp.where(odd == 0, below, above)
            is_far = jnp.where(odd == 0, above, below)
            near_ref[frame, near_count] = local
            far_ref[frame, far_count] = local
            place = jnp.where(is_near == 1, blocks + near_count, local)
            table_ref[frame, block] = jnp.where(is_far == 1, blocks + slots + far_count, place)
            return near_count + is_near, far_count + is_far

        lax.fori_loop(0, blocks, visit, (jnp.int32(0), jnp.int32(0)))
    for copy in copies:
        copy.wait()


def weights_kernel(merging_ref, first_ref, second_ref, feat_out, warp_out, first_out, second_out):
    chans = first_ref.shape[2]
    depth = 3 * chans
    for source, start, out in (
        (merging_ref, 0, feat_out),
        (merging_ref, chans, warp_out),
        (first_ref, 0, first_out),
        (second_ref, 0, second_out),
    ):
        width = source.shape[3]
        zero = jnp.zeros((chans, width), BF16)
        for a in range(4):
            for e in range(3):
                top = a * depth + e * chans
                for half in range(2):
                    tap = a - half
                    if 0 <= tap < 3:
                        value = source[tap, e, start:start + chans, :]
                    else:
                        value = zero
                    out[top:top + chans, half * width:(half + 1) * width] = value


def pack(pool_ref, near_list, far_list, frame, near_out, far_out):
    for slot in range(near_out.shape[0]):
        near_out[slot] = pool_ref[near_list[frame, slot]]
        far_out[slot] = pool_ref[far_list[frame, slot]]


def pack_kernel(frame, state_ref, near_list, far_list, pool_out, near_out, far_out):
    band, _, across = state_ref.shape[:3]
    for q in range(band):
        for r in range(BLK):
            pool_out[q * across:(q + 1) * across, r] = state_ref[q, r]
    pack(pool_out, near_list, far_list, frame, near_out, far_out)


def spread(out_ref, pair, half, value, cols):
    chans = value.shape[1]
    pairs = value.shape[0] // cols
    place = lax.broadcasted_iota(jnp.int32, (pairs, cols, chans), 1).reshape(value.shape)
    left = jnp.where(place == 0, 0.0, pltpu.roll(value, 1, 0))
    right = jnp.where(place == cols - 1, 0.0, pltpu.roll(value, value.shape[0] - 1, 0))
    for e, part in enumerate((left, value, right)):
        out_ref[pair:pair + pairs, half, :, e * chans:(e + 1) * chans] = (
            part.astype(BF16).reshape(pairs, cols, chans)
        )


def pair_dot(x_ref, w_ref, pair, pairs):
    cols, depth = x_ref.shape[2:]
    parts = [
        x_ref[pair + a // 2:pair + a // 2 + pairs, a % 2].reshape(pairs * cols, depth)
        for a in range(4)
    ]
    return jnp.dot(jnp.concatenate(parts, axis=1), w_ref[...], preferred_element_type=F32)


def chunks(total, size):
    return [(start, min(size, total - start)) for start in range(0, total, size)]


def load_rows(x_out, get_row, total, cols):
    for row in range(total):
        spread(x_out, row // 2, row % 2, get_row(row), cols)


def features_kernel(frame, place_ref, feat_ref, near_ref, far_ref, w_ref, out_ref, x_ref):
    rows, across, _, chans = feat_ref.shape[1:]
    cols = across * BLK
    even = lax.rem(place_ref[0], 2) == 0

    def get_row(row):
        row -= HALO
        if row < 0:
            value = jnp.where(even, far_ref[frame, row + HALO], near_ref[frame, row + HALO])
        elif row >= rows:
            value = jnp.where(even, near_ref[frame, row - rows], far_ref[frame, row - rows])
        else:
            value = feat_ref[frame, row]
        return value.astype(F32).reshape(cols, chans)

    load_rows(x_ref, get_row, rows + 2 * HALO, cols)
    for pair, pairs in chunks(rows // 2 + 2, 2):
        out_ref[pair:pair + pairs] = pair_dot(x_ref, w_ref, pair, pairs).reshape(
            pairs, cols, out_ref.shape[2]
        )


def assemble_kernel(frame, place_ref, table_ref, pool_ref, near_ref, far_ref,
                    warped_out, near_edge, far_edge, all_ref):
    rows, across = warped_out.shape[:2]
    blocks = pool_ref.shape[0]
    slots = near_ref.shape[0]
    all_ref[0:blocks] = pool_ref[...]
    all_ref[blocks:blocks + slots] = near_ref[...]
    all_ref[blocks + slots:blocks + 2 * slots] = far_ref[...]
    for block in range(blocks):
        q, p = divmod(block, across)
        warped_out[q * BLK:(q + 1) * BLK, p] = all_ref[table_ref[frame, block]]
    odd = lax.rem(place_ref[0], 2)
    near_start = jnp.where(odd == 0, rows - HALO, 0)
    far_start = jnp.where(odd == 0, 0, rows - HALO)
    near_edge[...] = warped_out[pl.ds(near_start, HALO)]
    far_edge[...] = warped_out[pl.ds(far_start, HALO)]


def main_kernel(frame, last, place_ref, part_ref, warped_ref, near_ref, far_ref, w1_ref, w2_ref, w3_ref,
                *refs):
    if last:
        _, out_ref, x_ref, m_ref, d_ref, state_ref, sem = refs
    else:
        near_list, far_list, out_ref, pool_out, near_out, far_out, x_ref, m_ref, d_ref, state_ref, sem = refs
    rows, across, _, chans = warped_ref.shape
    cols = across * BLK
    mine = place_ref[0]
    even = lax.rem(mine, 2) == 0
    has_above = mine > 0
    has_below = (mine + 1) * (rows // BLK) < place_ref[1]

    def get_row(row):
        row -= HALO
        if row < 0:
            value = jnp.where(even, far_ref[row + HALO], near_ref[row + HALO])
        elif row >= rows:
            value = jnp.where(even, near_ref[row - rows], far_ref[row - rows])
        else:
            value = warped_ref[row]
        return value.astype(F32).reshape(cols, chans)

    load_rows(x_ref, get_row, rows + 2 * HALO, cols)

    def keep(value, row):
        if row < 0:
            return jnp.where(has_above, value, 0.0)
        if row >= rows:
            return jnp.where(has_below, value, 0.0)
        return value

    step = 2
    for pair, pairs in chunks(rows // 2 + 2, step):
        raw = part_ref[pair:pair + pairs].reshape(pairs * cols, 2 * chans)
        raw = raw + pair_dot(x_ref, w1_ref, pair, pairs)
        value = jnp.maximum(raw, 0.1 * raw)
        for n in range(pairs):
            for half in range(2):
                one = value[n * cols:(n + 1) * cols, half * chans:(half + 1) * chans]
                spread(m_ref, pair + n, half, keep(one, 2 * (pair + n) + half - 2), cols)
    for pair, pairs in chunks(rows // 2 + 1, step):
        value = jnp.maximum(pair_dot(m_ref, w2_ref, pair, pairs), 0.0)
        for n in range(pairs):
            for half in range(2):
                one = value[n * cols:(n + 1) * cols, half * chans:(half + 1) * chans]
                spread(d_ref, pair + n, half, keep(one, 2 * (pair + n) + half - 1), cols)
    copies = []
    for pair, pairs in chunks(rows // 2, step):
        value = pair_dot(d_ref, w3_ref, pair, pairs)
        for n in range(pairs):
            for half in range(2):
                row = 2 * (pair + n) + half
                one = value[n * cols:(n + 1) * cols, half * chans:(half + 1) * chans]
                centre = m_ref[pair + n + 1, half, :, chans:2 * chans].astype(F32)
                done = (centre + one).reshape(across, BLK, chans).astype(BF16)
                state_ref[row] = done
                if not last:
                    q, r = divmod(row, BLK)
                    pool_out[q * across:(q + 1) * across, r] = done
        copy = pltpu.make_async_copy(
            state_ref.at[pl.ds(2 * pair, 2 * pairs)],
            out_ref.at[frame, pl.ds(2 * pair, 2 * pairs)],
            sem,
        )
        copy.start()
        copies.append(copy)
    if not last:
        pack(pool_out, near_list, far_list, frame + 1, near_out, far_out)
    pltpu.make_async_copy(state_ref, out_ref.at[frame], sem).wait()


def on_device(state_start, features, row_moves, col_moves, merging_weight, first_weight, second_weight):
    rows, cols, chans = state_start.shape
    frames = features.shape[0]
    band = rows // BLK
    across = cols // BLK
    blocks = band * across
    slots = blocks // 2
    list_len = slots + 8
    mine = lax.axis_index("rows")
    place = jnp.stack([mine, jnp.int32(band * lax.axis_size("rows"))]).astype(jnp.int32)
    state = state_start.reshape(band, BLK, across, BLK, chans)
    feats = features.reshape(frames, rows, across, BLK, chans)
    block_shape = (BLK, BLK, chans)
    edge_shape = (HALO, across, BLK, chans)

    table, near_list, far_list, near_feat, far_feat = pl.pallas_call(
        functools.partial(tables_kernel, band, across, slots),
        out_shape=[
            shape_of((frames, blocks), jnp.int32),
            shape_of((frames, list_len), jnp.int32),
            shape_of((frames, list_len), jnp.int32),
            shape_of((frames,) + edge_shape),
            shape_of((frames,) + edge_shape),
        ],
        in_specs=[SMEM, SMEM, SMEM, ANY],
        out_specs=[SMEM, SMEM, SMEM, VMEM, VMEM],
        scratch_shapes=[pltpu.SemaphoreType.DMA((2,))],
        name="tables",
    )(place, row_moves, col_moves, feats)
    near_list, far_list = swap_both(near_list, far_list)
    near_feat, far_feat = swap_both(near_feat, far_feat)

    pair_shape = shape_of((4 * 3 * chans, 2 * chans))
    w_feat, w_warp, w_first, w_second = pl.pallas_call(
        weights_kernel,
        out_shape=[pair_shape] * 4,
        in_specs=[VMEM] * 3,
        out_specs=[VMEM] * 4,
        name="weights",
    )(merging_weight, first_weight, second_weight)

    pool_shape = shape_of((blocks,) + block_shape)
    message = shape_of((slots,) + block_shape)
    pool, near_msg, far_msg = pl.pallas_call(
        functools.partial(pack_kernel, 0),
        out_shape=[pool_shape, message, message],
        in_specs=[VMEM, SMEM, SMEM],
        out_specs=[VMEM] * 3,
        name="pack",
    )(state, near_list, far_list)

    def wide(extra):
        return pltpu.VMEM((rows // 2 + extra, 2, cols, 3 * chans), BF16)

    def features_part(frame):
        return pl.pallas_call(
            functools.partial(features_kernel, frame),
            out_shape=shape_of((rows // 2 + 2, cols, 2 * chans), F32),
            in_specs=[SMEM] + [VMEM] * 4,
            out_specs=VMEM,
            scratch_shapes=[wide(3)],
            name="features",
        )(place, feats, near_feat, far_feat, w_feat)

    out = None
    out_shape = shape_of((frames, rows, across, BLK, chans))
    for frame in range(frames):
        last = frame == frames - 1
        part = features_part(frame)
        near_got, far_got = swap_both(near_msg, far_msg)
        warped, near_edge, far_edge = pl.pallas_call(
            functools.partial(assemble_kernel, frame),
            out_shape=[shape_of((rows, across, BLK, chans)), shape_of(edge_shape), shape_of(edge_shape)],
            in_specs=[SMEM, SMEM] + [VMEM] * 3,
            out_specs=[VMEM] * 3,
            scratch_shapes=[pltpu.VMEM((blocks + 2 * slots,) + block_shape, BF16)],
            name="assemble",
        )(place, table, pool, near_got, far_got)
        near_halo, far_halo = swap_both(near_edge, far_edge)
        scratch = [
            wide(3),
            wide(2),
            wide(1),
            pltpu.VMEM((rows, across, BLK, chans), BF16),
            pltpu.SemaphoreType.DMA,
        ]
        args = (place, part, warped, near_halo, far_halo, w_warp, w_first, w_second)
        kernel = functools.partial(main_kernel, frame, last)
        if last:
            out = pl.pallas_call(
                kernel,
                out_shape=out_shape,
                in_specs=[SMEM] + [VMEM] * 7 + [ANY],
                out_specs=ANY,
                input_output_aliases={8: 0},
                scratch_shapes=scratch,
                name="frame",
            )(*args, out)
        else:
            out, pool, near_msg, far_msg = pl.pallas_call(
                kernel,
                out_shape=[out_shape, pool_shape, message, message],
                in_specs=[SMEM] + [VMEM] * 7 + [SMEM] * 2,
                out_specs=[ANY] + [VMEM] * 3,
                scratch_shapes=scratch,
                name="frame",
            )(*args, near_list, far_list)
    return out.reshape(frames, rows, cols, chans)


def solution(mesh):
    in_specs = (
        P(("clips", "rows"), None, None),
        P(None, ("clips", "rows"), None, None),
        P(None, ("clips", "rows")),
        P(None, ("clips", "rows")),
        P(),
        P(),
        P(),
    )
    out_specs = P(None, ("clips", "rows"), None, None)
    return jax.shard_map(
        on_device, mesh=mesh, in_specs=in_specs, out_specs=out_specs, check_vma=False
    )
```

```python
import functools

import jax
import jax.numpy as jnp
from jax import lax
from jax.experimental import pallas as pl
from jax.experimental.pallas import tpu as pltpu
from jax.sharding import PartitionSpec as P


BLK = 8
HALO = 3
STEP = 4
VMEM = pl.BlockSpec(memory_space=pltpu.VMEM)
SMEM = pl.BlockSpec(memory_space=pltpu.SMEM)
ANY = pl.BlockSpec(memory_space=pl.ANY)
BF16 = jnp.bfloat16
F32 = jnp.float32


def shape_of(shape, dtype=BF16):
    return jax.ShapeDtypeStruct(shape, dtype)


def on_chip(shape, dtype=BF16):
    return pltpu.VMEM(shape, dtype)


def room(mebibytes):
    return pltpu.CompilerParams(vmem_limit_bytes=mebibytes << 20)


def in_hbm(x):
    return pltpu.with_memory_space_constraint(x, pltpu.HBM)


def resident(x):
    return pltpu.with_memory_space_constraint(x, pltpu.VMEM)


def swap(x, axis, first):
    size = lax.axis_size(axis)
    pairs = []
    for i in range(first, size - 1, 2):
        pairs += [(i, i + 1), (i + 1, i)]
    return lax.ppermute(x, axis, pairs)


def swap_both(for_even, for_odd):
    far = swap(for_odd, "rows", 1)
    near = swap(for_even, "rows", 0)
    return near, far


def tables_kernel(band, across, slots, place_ref, row_hbm, col_hbm, feat_hbm,
                  table_ref, near_ref, far_ref, near_edge, far_edge, row_ref, col_ref, sem):
    frames, blocks = row_ref.shape
    rows = feat_hbm.shape[1]
    mine = place_ref[0]
    total = place_ref[1]
    even = lax.rem(mine, 2) == 0
    moves = [
        pltpu.make_async_copy(row_hbm, row_ref, sem.at[0]),
        pltpu.make_async_copy(col_hbm, col_ref, sem.at[1]),
    ]
    near_rows = pl.ds(jnp.where(even, rows - HALO, 0), HALO)
    far_rows = pl.ds(jnp.where(even, 0, rows - HALO), HALO)
    edges = [
        pltpu.make_async_copy(feat_hbm.at[:, near_rows], near_edge, sem.at[2]),
        pltpu.make_async_copy(feat_hbm.at[:, far_rows], far_edge, sem.at[3]),
    ]
    for copy in moves + edges:
        copy.start()
    for copy in moves:
        copy.wait()
    block = lax.broadcasted_iota(jnp.int32, (frames, blocks), 1)
    source = jnp.clip(block // across + row_ref[...], -mine * band, total - 1 - mine * band)
    column = jnp.clip(block % across + col_ref[...], 0, across - 1)
    above = source < 0
    below = source >= band
    local = source * across + column + jnp.where(above, blocks, jnp.where(below, -blocks, 0))
    earlier = lax.broadcasted_iota(jnp.int32, (blocks, blocks), 0) < lax.broadcasted_iota(
        jnp.int32, (blocks, blocks), 1
    )
    earlier = jnp.where(earlier, 1.0, 0.0).astype(BF16)

    def rank(mask):
        ones = jnp.where(mask, 1.0, 0.0).astype(BF16)
        return jnp.dot(ones, earlier, preferred_element_type=F32).astype(jnp.int32)

    rank_above = rank(above)
    rank_below = rank(below)
    near_base = blocks
    far_base = blocks + slots
    above_base = jnp.where(even, far_base, near_base)
    below_base = jnp.where(even, near_base, far_base)
    table = jnp.where(above, above_base + rank_above, local)
    table_ref[...] = jnp.where(below, below_base + rank_below, table)
    near_rank = jnp.where(even, jnp.where(below, rank_below, -1), jnp.where(above, rank_above, -1))
    far_rank = jnp.where(even, jnp.where(above, rank_above, -1), jnp.where(below, rank_below, -1))
    length = near_ref.shape[1]
    slot = lax.broadcasted_iota(jnp.int32, (length, blocks), 0)
    for frame in range(frames):
        ids = local[frame:frame + 1].astype(F32).astype(BF16)
        for ranks, out in ((near_rank, near_ref), (far_rank, far_ref)):
            chosen = jnp.where(ranks[frame:frame + 1] == slot, 1.0, 0.0).astype(BF16)
            got = lax.dot_general(ids, chosen, (((1,), (1,)), ((), ())), preferred_element_type=F32)
            out[frame:frame + 1] = got.astype(jnp.int32)
    for copy in edges:
        copy.wait()


def prepare_kernel(merging_hbm, first_hbm, second_hbm, state_hbm,
                   feat_out, warp_out, first_out, second_out, pool_out,
                   merging_ref, first_ref, second_ref, sem):
    band, _, across = state_hbm.shape[:3]
    for q in range(band):
        for r in range(BLK):
            pltpu.make_async_copy(
                state_hbm.at[q, r], pool_out.at[pl.ds(q * across, across), r], sem.at[3]
            ).start()
    loads = [
        pltpu.make_async_copy(merging_hbm, merging_ref, sem.at[0]),
        pltpu.make_async_copy(first_hbm, first_ref, sem.at[1]),
        pltpu.make_async_copy(second_hbm, second_ref, sem.at[2]),
    ]
    for load in loads:
        load.start()
    chans = first_ref.shape[2]
    depth = 3 * chans
    for source, start, out, load in (
        (merging_ref, 0, feat_out, loads[0]),
        (merging_ref, chans, warp_out, None),
        (first_ref, 0, first_out, loads[1]),
        (second_ref, 0, second_out, loads[2]),
    ):
        if load is not None:
            load.wait()
        width = source.shape[3]
        zero = jnp.zeros((chans, width), BF16)
        for a in range(4):
            for e in range(3):
                top = a * depth + e * chans
                for half in range(2):
                    tap = a - half
                    if 0 <= tap < 3:
                        value = source[tap, e, start:start + chans, :]
                    else:
                        value = zero
                    out[top:top + chans, half * width:(half + 1) * width] = value
    pltpu.make_async_copy(pool_out, pool_out, sem.at[3]).wait()


def pack(pool_ref, near_list, far_list, frame, near_out, far_out):
    for slot in range(near_out.shape[0]):
        near_out[slot] = pool_ref[near_list[frame, slot]]
        far_out[slot] = pool_ref[far_list[frame, slot]]


def pack_kernel(frame, pool_ref, near_list, far_list, near_out, far_out):
    pack(pool_ref, near_list, far_list, frame, near_out, far_out)


def spread(out_ref, pair, half, value, cols):
    chans = value.shape[1]
    pairs = value.shape[0] // cols
    place = lax.broadcasted_iota(jnp.int32, (pairs, cols, chans), 1).reshape(value.shape)
    left = jnp.where(place == 0, 0.0, pltpu.roll(value, 1, 0))
    right = jnp.where(place == cols - 1, 0.0, pltpu.roll(value, value.shape[0] - 1, 0))
    for e, part in enumerate((left, value, right)):
        out_ref[pair:pair + pairs, half, :, e * chans:(e + 1) * chans] = (
            part.astype(BF16).reshape(pairs, cols, chans)
        )


def pair_dot(x_ref, w_ref, pair, pairs):
    cols, depth = x_ref.shape[2:]
    parts = [
        x_ref[pair + a // 2:pair + a // 2 + pairs, a % 2].reshape(pairs * cols, depth)
        for a in range(4)
    ]
    return jnp.dot(jnp.concatenate(parts, axis=1), w_ref[...], preferred_element_type=F32)


def chunks(first, end, size):
    total = end - first
    count = -(-total // size)
    bounds = [first + total * n // count for n in range(count + 1)]
    return [(a, b - a) for a, b in zip(bounds, bounds[1:])]


def features_kernel(frame, place_ref, feat_hbm, near_ref, far_ref, w_ref, out_ref, feat_ref, x_ref, sem):
    rows, across, _, chans = feat_ref.shape
    cols = across * BLK
    even = lax.rem(place_ref[0], 2) == 0
    size = rows // sem.shape[0]
    loads = []
    for n in range(sem.shape[0]):
        part = pl.ds(n * size, size)
        loads.append(pltpu.make_async_copy(feat_hbm.at[frame, part], feat_ref.at[part], sem.at[n]))
        loads[-1].start()
    for row in range(-HALO, rows + HALO):
        if row < 0:
            value = jnp.where(even, far_ref[frame, row + HALO], near_ref[frame, row + HALO])
        elif row >= rows:
            value = jnp.where(even, near_ref[frame, row - rows], far_ref[frame, row - rows])
        else:
            if row % size == 0:
                loads[row // size].wait()
            value = feat_ref[row]
        value = value.astype(F32).reshape(cols, chans)
        spread(x_ref, (row + HALO) // 2, (row + HALO) % 2, value, cols)
    for pair, pairs in chunks(0, rows // 2 + 2, STEP):
        out_ref[pair:pair + pairs] = pair_dot(x_ref, w_ref, pair, pairs).reshape(
            pairs, cols, out_ref.shape[2]
        )


def assemble_kernel(frame, place_ref, table_ref, pool_ref, near_ref, far_ref, _,
                    warped_out, near_edge, far_edge, all_ref):
    rows, across = warped_out.shape[:2]
    blocks = pool_ref.shape[0]
    slots = near_ref.shape[0]
    all_ref[0:blocks] = pool_ref[...]
    all_ref[blocks:blocks + slots] = near_ref[...]
    all_ref[blocks + slots:blocks + 2 * slots] = far_ref[...]
    for block in range(blocks):
        q, p = divmod(block, across)
        warped_out[q * BLK:(q + 1) * BLK, p] = all_ref[table_ref[frame, block]]
    odd = lax.rem(place_ref[0], 2)
    near_start = jnp.where(odd == 0, rows - HALO, 0)
    far_start = jnp.where(odd == 0, 0, rows - HALO)
    near_edge[...] = warped_out[pl.ds(near_start, HALO)]
    far_edge[...] = warped_out[pl.ds(far_start, HALO)]


def split_rows(value, pairs, cols, chans):
    for n in range(pairs):
        for half in range(2):
            yield n, half, value[n * cols:(n + 1) * cols, half * chans:(half + 1) * chans]


def finish(state_ref, pool_ref, centre, value, row, across, chans):
    done = (centre.astype(F32) + value).reshape(across, BLK, chans).astype(BF16)
    state_ref[row] = done
    if pool_ref is not None:
        q, r = divmod(row, BLK)
        pool_ref[q * across:(q + 1) * across, r] = done


def inner_kernel(frame, last, part_ref, warped_ref, w1_ref, w2_ref, w3_ref, *refs):
    if frame:
        refs = refs[1:]
    out_ref = refs[0]
    pool_ref = None if last else refs[1]
    m_edge, d_edge, x_ref, m_ref, d_ref, state_ref, sem = refs[-7:]
    rows, across, _, chans = warped_ref.shape
    cols = across * BLK
    half_rows = rows // 2
    for row in range(rows):
        value = warped_ref[row].astype(F32).reshape(cols, chans)
        spread(x_ref, (row + HALO) // 2, (row + HALO) % 2, value, cols)
    for pair, pairs in chunks(2, half_rows, STEP):
        raw = part_ref[pair:pair + pairs].reshape(pairs * cols, 2 * chans)
        raw = raw + pair_dot(x_ref, w1_ref, pair, pairs)
        value = jnp.maximum(raw, 0.1 * raw)
        for n, half, one in split_rows(value, pairs, cols, chans):
            spread(m_ref, pair + n, half, one, cols)
    m_edge[0] = m_ref[2]
    m_edge[1] = m_ref[half_rows - 1]
    for pair, pairs in chunks(2, half_rows - 1, STEP):
        value = jnp.maximum(pair_dot(m_ref, w2_ref, pair, pairs), 0.0)
        for n, half, one in split_rows(value, pairs, cols, chans):
            spread(d_ref, pair + n, half, one, cols)
    d_edge[0] = d_ref[2]
    d_edge[1] = d_ref[half_rows - 2]
    for pair, pairs in chunks(2, half_rows - 2, STEP):
        value = pair_dot(d_ref, w3_ref, pair, pairs)
        for n, half, one in split_rows(value, pairs, cols, chans):
            centre = m_ref[pair + n + 1, half, :, chans:2 * chans]
            finish(state_ref, pool_ref, centre, one, 2 * (pair + n) + half, across, chans)
        pltpu.make_async_copy(
            state_ref.at[pl.ds(2 * pair, 2 * pairs)],
            out_ref.at[frame, pl.ds(2 * pair, 2 * pairs)],
            sem,
        ).start()
    inner = pl.ds(4, rows - 8)
    pltpu.make_async_copy(state_ref.at[inner], out_ref.at[frame, inner], sem).wait()


def border_kernel(frame, last, place_ref, part_ref, warped_ref, near_ref, far_ref, w1_ref, w2_ref, w3_ref,
                  m_edge, d_edge, *refs):
    if last:
        _, out_ref, x_ref, m_ref, d_ref, state_ref, sem = refs
        pool_ref = None
    else:
        _, _, near_list, far_list, out_ref, pool_ref, near_out, far_out = refs[:8]
        x_ref, m_ref, d_ref, state_ref, sem = refs[8:]
    rows, across, _, chans = warped_ref.shape
    cols = across * BLK
    mine = place_ref[0]
    even = lax.rem(mine, 2) == 0
    has_above = mine > 0
    has_below = (mine + 1) * (rows // BLK) < place_ref[1]
    depth = 3 * chans

    def edge_dot(ref, side, w_ref):
        parts = [ref[side, a // 2:a // 2 + 2, a % 2].reshape(2 * cols, depth) for a in range(4)]
        return jnp.dot(jnp.concatenate(parts, axis=1), w_ref[...], preferred_element_type=F32)

    def flat(value):
        return value.astype(F32).reshape(cols, chans)

    for n in range(HALO):
        above = jnp.where(even, far_ref[n], near_ref[n])
        below = jnp.where(even, near_ref[n], far_ref[n])
        spread(x_ref.at[0], n // 2, n % 2, flat(above), cols)
        spread(x_ref.at[0], (n + 3) // 2, (n + 3) % 2, flat(warped_ref[n]), cols)
        spread(x_ref.at[1], n // 2, n % 2, flat(warped_ref[rows - HALO + n]), cols)
        spread(x_ref.at[1], (n + 3) // 2, (n + 3) % 2, flat(below), cols)
    half_rows = rows // 2

    def masked(value, row):
        if row < 0:
            return jnp.where(has_above, value, 0.0)
        return jnp.where(has_below, value, 0.0) if row >= rows else value

    m_ref[0, 2] = m_edge[0]
    m_ref[1, 0] = m_edge[1]
    d_ref[0, 2] = d_edge[0]
    d_ref[1, 0] = d_edge[1]
    for side in range(2):
        first = side * half_rows
        raw = part_ref[first:first + 2].reshape(2 * cols, 2 * chans) + edge_dot(x_ref, side, w1_ref)
        value = jnp.maximum(raw, 0.1 * raw)
        for n, half, one in split_rows(value, 2, cols, chans):
            one = masked(one, 2 * (first + n) + half - 2)
            spread(m_ref.at[side], n + side, half, one, cols)
    for side in range(2):
        first = side * (half_rows - 1)
        value = jnp.maximum(edge_dot(m_ref, side, w2_ref), 0.0)
        for n, half, one in split_rows(value, 2, cols, chans):
            one = masked(one, 2 * (first + n) + half - 1)
            spread(d_ref.at[side], n + side, half, one, cols)
    for side in range(2):
        first = side * (half_rows - 2)
        value = edge_dot(d_ref, side, w3_ref)
        for n, half, one in split_rows(value, 2, cols, chans):
            centre = m_ref[side, n + 1 - side, half, :, chans:2 * chans]
            finish(state_ref, pool_ref, centre, one, 2 * (first + n) + half, across, chans)
    copies = []
    for n, start in enumerate((0, rows - 4)):
        part = pl.ds(start, 4)
        copies.append(pltpu.make_async_copy(state_ref.at[part], out_ref.at[frame, part], sem.at[n]))
        copies[-1].start()
    if not last:
        pack(pool_ref, near_list, far_list, frame + 1, near_out, far_out)
    for copy in copies:
        copy.wait()


def on_device(state_start, features, row_moves, col_moves, merging_weight, first_weight, second_weight):
    rows, cols, chans = state_start.shape
    frames = features.shape[0]
    band = rows // BLK
    across = cols // BLK
    blocks = band * across
    slots = blocks // 2
    list_len = slots + 8
    mine = lax.axis_index("rows")
    place = jnp.stack([mine, jnp.int32(band * lax.axis_size("rows"))]).astype(jnp.int32)
    state = state_start.reshape(band, BLK, across, BLK, chans)
    feats = features.reshape(frames, rows, across, BLK, chans)
    block_shape = (BLK, BLK, chans)
    edge_shape = (HALO, across, BLK, chans)

    table, near_list, far_list, near_feat, far_feat = pl.pallas_call(
        functools.partial(tables_kernel, band, across, slots),
        out_shape=[
            on_chip((frames, blocks), jnp.int32),
            on_chip((frames, list_len), jnp.int32),
            on_chip((frames, list_len), jnp.int32),
            on_chip((frames,) + edge_shape),
            on_chip((frames,) + edge_shape),
        ],
        in_specs=[SMEM, ANY, ANY, ANY],
        out_specs=[VMEM] * 5,
        scratch_shapes=[
            pltpu.VMEM((frames, blocks), jnp.int32),
            pltpu.VMEM((frames, blocks), jnp.int32),
            pltpu.SemaphoreType.DMA((4,)),
        ],
        compiler_params=room(4),
        name="tables",
    )(place, *map(in_hbm, (row_moves, col_moves, feats)))
    near_list, far_list = swap_both(near_list, far_list)
    near_feat, far_feat = swap_both(near_feat, far_feat)

    pair_shape = on_chip((4 * 3 * chans, 2 * chans))
    pool_shape = on_chip((blocks,) + block_shape)
    message = on_chip((slots,) + block_shape)
    w_feat, w_warp, w_first, w_second, pool = pl.pallas_call(
        prepare_kernel,
        out_shape=[pair_shape] * 4 + [pool_shape],
        in_specs=[ANY] * 4,
        out_specs=[VMEM] * 5,
        scratch_shapes=[
            pltpu.VMEM(merging_weight.shape, BF16),
            pltpu.VMEM(first_weight.shape, BF16),
            pltpu.VMEM(second_weight.shape, BF16),
            pltpu.SemaphoreType.DMA((4,)),
        ],
        compiler_params=room(4),
        name="prepare",
    )(*map(in_hbm, (merging_weight, first_weight, second_weight, state)))

    near_msg, far_msg = pl.pallas_call(
        functools.partial(pack_kernel, 0),
        out_shape=[message, message],
        in_specs=[VMEM, SMEM, SMEM],
        out_specs=[VMEM] * 2,
        compiler_params=room(4),
        name="pack",
    )(resident(pool), near_list, far_list)

    def wide(extra):
        return pltpu.VMEM((rows // 2 + extra, 2, cols, 3 * chans), BF16)

    def features_part(frame):
        return pl.pallas_call(
            functools.partial(features_kernel, frame),
            out_shape=on_chip((rows // 2 + 2, cols, 2 * chans), F32),
            in_specs=[SMEM, ANY] + [VMEM] * 3,
            out_specs=VMEM,
            scratch_shapes=[
                pltpu.VMEM((rows, across, BLK, chans), BF16),
                wide(3),
                pltpu.SemaphoreType.DMA((4,)),
            ],
            compiler_params=room(16),
            name="features",
        )(place, in_hbm(feats), resident(near_feat), resident(far_feat), resident(w_feat))

    out = None
    out_shape = shape_of((frames, rows, across, BLK, chans))
    edge_pairs = on_chip((2, 2, cols, 3 * chans))
    for frame in range(frames):
        last = frame == frames - 1
        near_got, far_got = swap_both(near_msg, far_msg)
        part = features_part(frame)
        warped, near_edge, far_edge = pl.pallas_call(
            functools.partial(assemble_kernel, frame),
            out_shape=[on_chip((rows, across, BLK, chans)), on_chip(edge_shape), on_chip(edge_shape)],
            in_specs=[SMEM, SMEM] + [VMEM] * 3 + [ANY],
            out_specs=[VMEM] * 3,
            scratch_shapes=[pltpu.VMEM((blocks + 2 * slots,) + block_shape, BF16)],
            compiler_params=room(8),
            name="assemble",
        )(place, table, resident(pool), resident(near_got), resident(far_got), part)
        near_halo, far_halo = swap_both(near_edge, far_edge)
        args = tuple(map(resident, (part, warped, w_warp, w_first, w_second)))
        results = pl.pallas_call(
            functools.partial(inner_kernel, frame, last),
            out_shape=[out_shape] + [pool_shape] * (not last) + [edge_pairs] * 2,
            in_specs=[VMEM] * 5 + [ANY] * (frame > 0),
            out_specs=[ANY] + [VMEM] * (2 + (not last)),
            input_output_aliases={5: 0} if frame else {},
            scratch_shapes=[
                wide(3),
                wide(2),
                wide(1),
                pltpu.VMEM((rows, across, BLK, chans), BF16),
                pltpu.SemaphoreType.DMA,
            ],
            compiler_params=room(24),
            name="inner",
        )(*args, *([out] if frame else []))
        out = results[0]
        m_edge, d_edge = results[-2:]
        args = (place,) + tuple(map(resident, (
            part, warped, near_halo, far_halo, w_warp, w_first, w_second, m_edge, d_edge
        )))
        scratch = [pltpu.VMEM((2, 3, 2, cols, 3 * chans), BF16) for _ in range(3)] + [
            pltpu.VMEM((rows, across, BLK, chans), BF16),
            pltpu.SemaphoreType.DMA((2,)),
        ]
        kernel = functools.partial(border_kernel, frame, last)
        if last:
            out = pl.pallas_call(
                kernel,
                out_shape=out_shape,
                in_specs=[SMEM] + [VMEM] * 9 + [ANY],
                out_specs=ANY,
                input_output_aliases={10: 0},
                scratch_shapes=scratch,
                compiler_params=room(12),
                name="border",
            )(*args, out)
        else:
            out, pool, near_msg, far_msg = pl.pallas_call(
                kernel,
                out_shape=[out_shape, pool_shape, message, message],
                in_specs=[SMEM] + [VMEM] * 9 + [ANY, VMEM] + [SMEM] * 2,
                out_specs=[ANY] + [VMEM] * 3,
                input_output_aliases={10: 0, 11: 1},
                scratch_shapes=scratch,
                compiler_params=room(12),
                name="border",
            )(*args, out, resident(results[1]), near_list, far_list)
    return out.reshape(frames, rows, cols, chans)


def solution(mesh):
    in_specs = (
        P(("clips", "rows"), None, None),
        P(None, ("clips", "rows"), None, None),
        P(None, ("clips", "rows")),
        P(None, ("clips", "rows")),
        P(),
        P(),
        P(),
    )
    out_specs = P(None, ("clips", "rows"), None, None)
    return jax.shard_map(
        on_device, mesh=mesh, in_specs=in_specs, out_specs=out_specs, check_vma=False
    )
```

```python
import functools

import jax
import jax.numpy as jnp
from jax import lax
from jax.experimental import pallas as pl
from jax.experimental.pallas import tpu as pltpu
from jax.sharding import PartitionSpec as P


BLK = 8
HALO = 3
STEP = 4
VMEM = pl.BlockSpec(memory_space=pltpu.VMEM)
SMEM = pl.BlockSpec(memory_space=pltpu.SMEM)
ANY = pl.BlockSpec(memory_space=pl.ANY)
BF16 = jnp.bfloat16
F32 = jnp.float32


def shape_of(shape, dtype=BF16):
    return jax.ShapeDtypeStruct(shape, dtype)


def on_chip(shape, dtype=BF16):
    return pltpu.VMEM(shape, dtype)


def room(mebibytes):
    return pltpu.CompilerParams(vmem_limit_bytes=mebibytes << 20)


def in_hbm(x):
    return pltpu.with_memory_space_constraint(x, pltpu.HBM)


def resident(x):
    return pltpu.with_memory_space_constraint(x, pltpu.VMEM)


def neighbours(first):
    clips, size = lax.axis_size("clips"), lax.axis_size("rows")
    inside = [(i, i + 1) for i in range(first, size - 1, 2)]
    pairs = [(c * size + i, c * size + j) for c in range(clips) for i, j in inside]
    left = [i for i in range(size) if not any(i in pair for pair in inside)]
    pairs += [(c * size + i, (c + 1) * size + i) for c in range(0, clips - 1, 2) for i in left]
    return pairs + [(j, i) for i, j in pairs]


def swap(x, first):
    return lax.ppermute(x, ("clips", "rows"), neighbours(first))


def swap_both(for_even, for_odd):
    far = swap(for_odd, 1)
    near = swap(for_even, 0)
    return near, far


def halo_row(near_row, far_row, even, exists, upper):
    row = jnp.where(even, far_row, near_row) if upper else jnp.where(even, near_row, far_row)
    return jnp.where(exists, row, jnp.zeros_like(row))


def borders(place_ref, band):
    mine = place_ref[0]
    return lax.rem(mine, 2) == 0, mine > 0, (mine + 1) * band < place_ref[1]


def tables_kernel(band, across, slots, place_ref, row_hbm, col_hbm, feat_hbm,
                  table_ref, near_ref, far_ref, near_edge, far_edge, row_ref, col_ref, sem):
    frames, blocks = row_ref.shape
    rows = feat_hbm.shape[1]
    mine = place_ref[0]
    total = place_ref[1]
    even = lax.rem(mine, 2) == 0
    moves = [
        pltpu.make_async_copy(row_hbm, row_ref, sem.at[0]),
        pltpu.make_async_copy(col_hbm, col_ref, sem.at[1]),
    ]
    near_rows = pl.ds(jnp.where(even, rows - HALO, 0), HALO)
    far_rows = pl.ds(jnp.where(even, 0, rows - HALO), HALO)
    edges = [
        pltpu.make_async_copy(feat_hbm.at[:, near_rows], near_edge, sem.at[2]),
        pltpu.make_async_copy(feat_hbm.at[:, far_rows], far_edge, sem.at[3]),
    ]
    for copy in moves + edges:
        copy.start()
    for copy in moves:
        copy.wait()
    block = lax.broadcasted_iota(jnp.int32, (frames, blocks), 1)
    source = jnp.clip(block // across + row_ref[...], -mine * band, total - 1 - mine * band)
    column = jnp.clip(block % across + col_ref[...], 0, across - 1)
    above = source < 0
    below = source >= band
    local = source * across + column + jnp.where(above, blocks, jnp.where(below, -blocks, 0))
    earlier = lax.broadcasted_iota(jnp.int32, (blocks, blocks), 0) < lax.broadcasted_iota(
        jnp.int32, (blocks, blocks), 1
    )
    earlier = jnp.where(earlier, 1.0, 0.0).astype(BF16)

    def rank(mask):
        ones = jnp.where(mask, 1.0, 0.0).astype(BF16)
        return jnp.dot(ones, earlier, preferred_element_type=F32).astype(jnp.int32)

    rank_above = rank(above)
    rank_below = rank(below)
    near_base = blocks
    far_base = blocks + slots
    above_base = jnp.where(even, far_base, near_base)
    below_base = jnp.where(even, near_base, far_base)
    table = jnp.where(above, above_base + rank_above, local)
    table_ref[...] = jnp.where(below, below_base + rank_below, table)
    near_rank = jnp.where(even, jnp.where(below, rank_below, -1), jnp.where(above, rank_above, -1))
    far_rank = jnp.where(even, jnp.where(above, rank_above, -1), jnp.where(below, rank_below, -1))
    length = near_ref.shape[1]
    slot = lax.broadcasted_iota(jnp.int32, (length, blocks), 0)
    for frame in range(frames):
        ids = local[frame:frame + 1].astype(F32).astype(BF16)
        for ranks, out in ((near_rank, near_ref), (far_rank, far_ref)):
            chosen = jnp.where(ranks[frame:frame + 1] == slot, 1.0, 0.0).astype(BF16)
            got = lax.dot_general(ids, chosen, (((1,), (1,)), ((), ())), preferred_element_type=F32)
            out[frame:frame + 1] = got.astype(jnp.int32)
    for copy in edges:
        copy.wait()


def prepare_kernel(merging_hbm, first_hbm, second_hbm, state_hbm,
                   feat_out, warp_out, first_out, second_out, pool_out,
                   merging_ref, first_ref, second_ref, sem):
    band, _, across = state_hbm.shape[:3]
    for q in range(band):
        for r in range(BLK):
            pltpu.make_async_copy(
                state_hbm.at[q, r], pool_out.at[pl.ds(q * across, across), r], sem.at[3]
            ).start()
    loads = [
        pltpu.make_async_copy(merging_hbm, merging_ref, sem.at[0]),
        pltpu.make_async_copy(first_hbm, first_ref, sem.at[1]),
        pltpu.make_async_copy(second_hbm, second_ref, sem.at[2]),
    ]
    for load in loads:
        load.start()
    chans = first_ref.shape[2]
    depth = 3 * chans
    for source, start, out, load in (
        (merging_ref, 0, feat_out, loads[0]),
        (merging_ref, chans, warp_out, None),
        (first_ref, 0, first_out, loads[1]),
        (second_ref, 0, second_out, loads[2]),
    ):
        if load is not None:
            load.wait()
        width = source.shape[3]
        zero = jnp.zeros((chans, width), BF16)
        for a in range(4):
            for e in range(3):
                top = a * depth + e * chans
                for half in range(2):
                    tap = a - half
                    if 0 <= tap < 3:
                        value = source[tap, e, start:start + chans, :]
                    else:
                        value = zero
                    out[top:top + chans, half * width:(half + 1) * width] = value
    pltpu.make_async_copy(pool_out, pool_out, sem.at[3]).wait()


def pack(pool_ref, near_list, far_list, frame, near_out, far_out):
    for slot in range(near_out.shape[0]):
        near_out[slot] = pool_ref[near_list[frame, slot]]
        far_out[slot] = pool_ref[far_list[frame, slot]]


def pack_kernel(frame, pool_ref, near_list, far_list, near_out, far_out):
    pack(pool_ref, near_list, far_list, frame, near_out, far_out)


def spread(out_ref, pair, half, value, cols):
    chans = value.shape[1]
    pairs = value.shape[0] // cols
    place = lax.broadcasted_iota(jnp.int32, (pairs, cols, chans), 1).reshape(value.shape)
    left = jnp.where(place == 0, 0.0, pltpu.roll(value, 1, 0))
    right = jnp.where(place == cols - 1, 0.0, pltpu.roll(value, value.shape[0] - 1, 0))
    for e, part in enumerate((left, value, right)):
        out_ref[pair:pair + pairs, half, :, e * chans:(e + 1) * chans] = (
            part.astype(BF16).reshape(pairs, cols, chans)
        )


def pair_dot(x_ref, w_ref, pair, pairs):
    cols, depth = x_ref.shape[2:]
    parts = [
        x_ref[pair + a // 2:pair + a // 2 + pairs, a % 2].reshape(pairs * cols, depth)
        for a in range(4)
    ]
    return jnp.dot(jnp.concatenate(parts, axis=1), w_ref[...], preferred_element_type=F32)


def chunks(first, end, size):
    total = end - first
    count = -(-total // size)
    bounds = [first + total * n // count for n in range(count + 1)]
    return [(a, b - a) for a, b in zip(bounds, bounds[1:])]


def features_kernel(frame, place_ref, feat_hbm, near_ref, far_ref, w_ref, out_ref, feat_ref, x_ref, sem):
    rows, across, _, chans = feat_ref.shape
    cols = across * BLK
    even, has_above, has_below = borders(place_ref, rows // BLK)
    size = rows // sem.shape[0]
    loads = []
    for n in range(sem.shape[0]):
        part = pl.ds(n * size, size)
        loads.append(pltpu.make_async_copy(feat_hbm.at[frame, part], feat_ref.at[part], sem.at[n]))
        loads[-1].start()
    for row in range(-HALO, rows + HALO):
        if row < 0:
            n = row + HALO
            value = halo_row(near_ref[frame, n], far_ref[frame, n], even, has_above, True)
        elif row >= rows:
            n = row - rows
            value = halo_row(near_ref[frame, n], far_ref[frame, n], even, has_below, False)
        else:
            if row % size == 0:
                loads[row // size].wait()
            value = feat_ref[row]
        value = value.astype(F32).reshape(cols, chans)
        spread(x_ref, (row + HALO) // 2, (row + HALO) % 2, value, cols)
    for pair, pairs in chunks(0, rows // 2 + 2, STEP):
        out_ref[pair:pair + pairs] = pair_dot(x_ref, w_ref, pair, pairs).reshape(
            pairs, cols, out_ref.shape[2]
        )


def assemble_kernel(frame, place_ref, table_ref, pool_ref, near_ref, far_ref, _,
                    warped_out, near_edge, far_edge, all_ref):
    rows, across = warped_out.shape[:2]
    blocks = pool_ref.shape[0]
    slots = near_ref.shape[0]
    all_ref[0:blocks] = pool_ref[...]
    all_ref[blocks:blocks + slots] = near_ref[...]
    all_ref[blocks + slots:blocks + 2 * slots] = far_ref[...]
    for block in range(blocks):
        q, p = divmod(block, across)
        warped_out[q * BLK:(q + 1) * BLK, p] = all_ref[table_ref[frame, block]]
    odd = lax.rem(place_ref[0], 2)
    near_start = jnp.where(odd == 0, rows - HALO, 0)
    far_start = jnp.where(odd == 0, 0, rows - HALO)
    near_edge[...] = warped_out[pl.ds(near_start, HALO)]
    far_edge[...] = warped_out[pl.ds(far_start, HALO)]


def split_rows(value, pairs, cols, chans):
    for n in range(pairs):
        for half in range(2):
            yield n, half, value[n * cols:(n + 1) * cols, half * chans:(half + 1) * chans]


def finish(state_ref, pool_ref, centre, value, row, across, chans):
    done = (centre.astype(F32) + value).reshape(across, BLK, chans).astype(BF16)
    state_ref[row] = done
    if pool_ref is not None:
        q, r = divmod(row, BLK)
        pool_ref[q * across:(q + 1) * across, r] = done


def inner_kernel(frame, last, part_ref, warped_ref, w1_ref, w2_ref, w3_ref, *refs):
    if frame:
        refs = refs[1:]
    out_ref = refs[0]
    pool_ref = None if last else refs[1]
    m_edge, d_edge, x_ref, m_ref, d_ref, state_ref, sem = refs[-7:]
    rows, across, _, chans = warped_ref.shape
    cols = across * BLK
    half_rows = rows // 2
    for row in range(rows):
        value = warped_ref[row].astype(F32).reshape(cols, chans)
        spread(x_ref, (row + HALO) // 2, (row + HALO) % 2, value, cols)
    for pair, pairs in chunks(2, half_rows, STEP):
        raw = part_ref[pair:pair + pairs].reshape(pairs * cols, 2 * chans)
        raw = raw + pair_dot(x_ref, w1_ref, pair, pairs)
        value = jnp.maximum(raw, 0.1 * raw)
        for n, half, one in split_rows(value, pairs, cols, chans):
            spread(m_ref, pair + n, half, one, cols)
    m_edge[0] = m_ref[2]
    m_edge[1] = m_ref[half_rows - 1]
    for pair, pairs in chunks(2, half_rows - 1, STEP):
        value = jnp.maximum(pair_dot(m_ref, w2_ref, pair, pairs), 0.0)
        for n, half, one in split_rows(value, pairs, cols, chans):
            spread(d_ref, pair + n, half, one, cols)
    d_edge[0] = d_ref[2]
    d_edge[1] = d_ref[half_rows - 2]
    for pair, pairs in chunks(2, half_rows - 2, STEP):
        value = pair_dot(d_ref, w3_ref, pair, pairs)
        for n, half, one in split_rows(value, pairs, cols, chans):
            centre = m_ref[pair + n + 1, half, :, chans:2 * chans]
            finish(state_ref, pool_ref, centre, one, 2 * (pair + n) + half, across, chans)
        pltpu.make_async_copy(
            state_ref.at[pl.ds(2 * pair, 2 * pairs)],
            out_ref.at[frame, pl.ds(2 * pair, 2 * pairs)],
            sem,
        ).start()
    inner = pl.ds(4, rows - 8)
    pltpu.make_async_copy(state_ref.at[inner], out_ref.at[frame, inner], sem).wait()


def border_kernel(frame, last, place_ref, part_ref, warped_ref, near_ref, far_ref, w1_ref, w2_ref, w3_ref,
                  m_edge, d_edge, *refs):
    if last:
        _, out_ref, x_ref, m_ref, d_ref, state_ref, sem = refs
        pool_ref = None
    else:
        _, _, near_list, far_list, out_ref, pool_ref, near_out, far_out = refs[:8]
        x_ref, m_ref, d_ref, state_ref, sem = refs[8:]
    rows, across, _, chans = warped_ref.shape
    cols = across * BLK
    even, has_above, has_below = borders(place_ref, rows // BLK)
    depth = 3 * chans

    def edge_dot(ref, side, w_ref):
        parts = [ref[side, a // 2:a // 2 + 2, a % 2].reshape(2 * cols, depth) for a in range(4)]
        return jnp.dot(jnp.concatenate(parts, axis=1), w_ref[...], preferred_element_type=F32)

    def flat(value):
        return value.astype(F32).reshape(cols, chans)

    for n in range(HALO):
        above = halo_row(near_ref[n], far_ref[n], even, has_above, True)
        below = halo_row(near_ref[n], far_ref[n], even, has_below, False)
        spread(x_ref.at[0], n // 2, n % 2, flat(above), cols)
        spread(x_ref.at[0], (n + 3) // 2, (n + 3) % 2, flat(warped_ref[n]), cols)
        spread(x_ref.at[1], n // 2, n % 2, flat(warped_ref[rows - HALO + n]), cols)
        spread(x_ref.at[1], (n + 3) // 2, (n + 3) % 2, flat(below), cols)
    half_rows = rows // 2

    def masked(value, row):
        if row < 0:
            return jnp.where(has_above, value, 0.0)
        return jnp.where(has_below, value, 0.0) if row >= rows else value

    m_ref[0, 2] = m_edge[0]
    m_ref[1, 0] = m_edge[1]
    d_ref[0, 2] = d_edge[0]
    d_ref[1, 0] = d_edge[1]
    for side in range(2):
        first = side * half_rows
        raw = part_ref[first:first + 2].reshape(2 * cols, 2 * chans) + edge_dot(x_ref, side, w1_ref)
        value = jnp.maximum(raw, 0.1 * raw)
        for n, half, one in split_rows(value, 2, cols, chans):
            one = masked(one, 2 * (first + n) + half - 2)
            spread(m_ref.at[side], n + side, half, one, cols)
    for side in range(2):
        first = side * (half_rows - 1)
        value = jnp.maximum(edge_dot(m_ref, side, w2_ref), 0.0)
        for n, half, one in split_rows(value, 2, cols, chans):
            one = masked(one, 2 * (first + n) + half - 1)
            spread(d_ref.at[side], n + side, half, one, cols)
    for side in range(2):
        first = side * (half_rows - 2)
        value = edge_dot(d_ref, side, w3_ref)
        for n, half, one in split_rows(value, 2, cols, chans):
            centre = m_ref[side, n + 1 - side, half, :, chans:2 * chans]
            finish(state_ref, pool_ref, centre, one, 2 * (first + n) + half, across, chans)
    copies = []
    for n, start in enumerate((0, rows - 4)):
        part = pl.ds(start, 4)
        copies.append(pltpu.make_async_copy(state_ref.at[part], out_ref.at[frame, part], sem.at[n]))
        copies[-1].start()
    if not last:
        pack(pool_ref, near_list, far_list, frame + 1, near_out, far_out)
    for copy in copies:
        copy.wait()


def on_device(state_start, features, row_moves, col_moves, merging_weight, first_weight, second_weight):
    rows, cols, chans = state_start.shape
    frames = features.shape[0]
    band = rows // BLK
    across = cols // BLK
    blocks = band * across
    slots = blocks // 2
    list_len = slots + 8
    mine = lax.axis_index("rows")
    place = jnp.stack([mine, jnp.int32(band * lax.axis_size("rows"))]).astype(jnp.int32)
    state = state_start.reshape(band, BLK, across, BLK, chans)
    feats = features.reshape(frames, rows, across, BLK, chans)
    block_shape = (BLK, BLK, chans)
    edge_shape = (HALO, across, BLK, chans)

    table, near_list, far_list, near_feat, far_feat = pl.pallas_call(
        functools.partial(tables_kernel, band, across, slots),
        out_shape=[
            on_chip((frames, blocks), jnp.int32),
            on_chip((frames, list_len), jnp.int32),
            on_chip((frames, list_len), jnp.int32),
            on_chip((frames,) + edge_shape),
            on_chip((frames,) + edge_shape),
        ],
        in_specs=[SMEM, ANY, ANY, ANY],
        out_specs=[VMEM] * 5,
        scratch_shapes=[
            pltpu.VMEM((frames, blocks), jnp.int32),
            pltpu.VMEM((frames, blocks), jnp.int32),
            pltpu.SemaphoreType.DMA((4,)),
        ],
        compiler_params=room(4),
        name="tables",
    )(place, *map(in_hbm, (row_moves, col_moves, feats)))
    near_list, far_list = swap_both(near_list, far_list)
    near_feat, far_feat = swap_both(near_feat, far_feat)

    pair_shape = on_chip((4 * 3 * chans, 2 * chans))
    pool_shape = on_chip((blocks,) + block_shape)
    message = on_chip((slots,) + block_shape)
    w_feat, w_warp, w_first, w_second, pool = pl.pallas_call(
        prepare_kernel,
        out_shape=[pair_shape] * 4 + [pool_shape],
        in_specs=[ANY] * 4,
        out_specs=[VMEM] * 5,
        scratch_shapes=[
            pltpu.VMEM(merging_weight.shape, BF16),
            pltpu.VMEM(first_weight.shape, BF16),
            pltpu.VMEM(second_weight.shape, BF16),
            pltpu.SemaphoreType.DMA((4,)),
        ],
        compiler_params=room(4),
        name="prepare",
    )(*map(in_hbm, (merging_weight, first_weight, second_weight, state)))

    near_msg, far_msg = pl.pallas_call(
        functools.partial(pack_kernel, 0),
        out_shape=[message, message],
        in_specs=[VMEM, SMEM, SMEM],
        out_specs=[VMEM] * 2,
        compiler_params=room(4),
        name="pack",
    )(resident(pool), near_list, far_list)

    def wide(extra):
        return pltpu.VMEM((rows // 2 + extra, 2, cols, 3 * chans), BF16)

    def features_part(frame):
        return pl.pallas_call(
            functools.partial(features_kernel, frame),
            out_shape=on_chip((rows // 2 + 2, cols, 2 * chans), F32),
            in_specs=[SMEM, ANY] + [VMEM] * 3,
            out_specs=VMEM,
            scratch_shapes=[
                pltpu.VMEM((rows, across, BLK, chans), BF16),
                wide(3),
                pltpu.SemaphoreType.DMA((4,)),
            ],
            compiler_params=room(16),
            name="features",
        )(place, in_hbm(feats), resident(near_feat), resident(far_feat), resident(w_feat))

    out = None
    out_shape = shape_of((frames, rows, across, BLK, chans))
    edge_pairs = on_chip((2, 2, cols, 3 * chans))
    for frame in range(frames):
        last = frame == frames - 1
        near_got, far_got = swap_both(near_msg, far_msg)
        part = features_part(frame)
        warped, near_edge, far_edge = pl.pallas_call(
            functools.partial(assemble_kernel, frame),
            out_shape=[on_chip((rows, across, BLK, chans)), on_chip(edge_shape), on_chip(edge_shape)],
            in_specs=[SMEM, SMEM] + [VMEM] * 3 + [ANY],
            out_specs=[VMEM] * 3,
            scratch_shapes=[pltpu.VMEM((blocks + 2 * slots,) + block_shape, BF16)],
            compiler_params=room(8),
            name="assemble",
        )(place, table, resident(pool), resident(near_got), resident(far_got), part)
        near_halo, far_halo = swap_both(near_edge, far_edge)
        args = tuple(map(resident, (part, warped, w_warp, w_first, w_second)))
        results = pl.pallas_call(
            functools.partial(inner_kernel, frame, last),
            out_shape=[out_shape] + [pool_shape] * (not last) + [edge_pairs] * 2,
            in_specs=[VMEM] * 5 + [ANY] * (frame > 0),
            out_specs=[ANY] + [VMEM] * (2 + (not last)),
            input_output_aliases={5: 0} if frame else {},
            scratch_shapes=[
                wide(3),
                wide(2),
                wide(1),
                pltpu.VMEM((rows, across, BLK, chans), BF16),
                pltpu.SemaphoreType.DMA,
            ],
            compiler_params=room(24),
            name="inner",
        )(*args, *([out] if frame else []))
        out = results[0]
        m_edge, d_edge = results[-2:]
        args = (place,) + tuple(map(resident, (
            part, warped, near_halo, far_halo, w_warp, w_first, w_second, m_edge, d_edge
        )))
        scratch = [pltpu.VMEM((2, 3, 2, cols, 3 * chans), BF16) for _ in range(3)] + [
            pltpu.VMEM((rows, across, BLK, chans), BF16),
            pltpu.SemaphoreType.DMA((2,)),
        ]
        kernel = functools.partial(border_kernel, frame, last)
        if last:
            out = pl.pallas_call(
                kernel,
                out_shape=out_shape,
                in_specs=[SMEM] + [VMEM] * 9 + [ANY],
                out_specs=ANY,
                input_output_aliases={10: 0},
                scratch_shapes=scratch,
                compiler_params=room(12),
                name="border",
            )(*args, out)
        else:
            out, pool, near_msg, far_msg = pl.pallas_call(
                kernel,
                out_shape=[out_shape, pool_shape, message, message],
                in_specs=[SMEM] + [VMEM] * 9 + [ANY, VMEM] + [SMEM] * 2,
                out_specs=[ANY] + [VMEM] * 3,
                input_output_aliases={10: 0, 11: 1},
                scratch_shapes=scratch,
                compiler_params=room(12),
                name="border",
            )(*args, out, resident(results[1]), near_list, far_list)
    return out.reshape(frames, rows, cols, chans)


def solution(mesh):
    in_specs = (
        P(("clips", "rows"), None, None),
        P(None, ("clips", "rows"), None, None),
        P(None, ("clips", "rows")),
        P(None, ("clips", "rows")),
        P(),
        P(),
        P(),
    )
    out_specs = P(None, ("clips", "rows"), None, None)
    return jax.shard_map(
        on_device, mesh=mesh, in_specs=in_specs, out_specs=out_specs, check_vma=False
    )
```

```python
import functools

import jax
import jax.numpy as jnp
from jax import lax
from jax.experimental import pallas as pl
from jax.experimental.pallas import tpu as pltpu
from jax.sharding import PartitionSpec as P


BLK = 8
HALO = 3
STEP = 4
VMEM = pl.BlockSpec(memory_space=pltpu.VMEM)
SMEM = pl.BlockSpec(memory_space=pltpu.SMEM)
ANY = pl.BlockSpec(memory_space=pl.ANY)
BF16 = jnp.bfloat16
F32 = jnp.float32


def shape_of(shape, dtype=BF16):
    return jax.ShapeDtypeStruct(shape, dtype)


def on_chip(shape, dtype=BF16):
    return pltpu.VMEM(shape, dtype)


def room(mebibytes):
    return pltpu.CompilerParams(vmem_limit_bytes=mebibytes << 20)


def in_hbm(x):
    return pltpu.with_memory_space_constraint(x, pltpu.HBM)


def resident(x):
    return pltpu.with_memory_space_constraint(x, pltpu.VMEM)


def neighbours(first):
    clips, size = lax.axis_size("clips"), lax.axis_size("rows")
    inside = [(i, i + 1) for i in range(first, size - 1, 2)]
    pairs = [(c * size + i, c * size + j) for c in range(clips) for i, j in inside]
    left = [i for i in range(size) if not any(i in pair for pair in inside)]
    pairs += [(c * size + i, (c + 1) * size + i) for c in range(0, clips - 1, 2) for i in left]
    return pairs + [(j, i) for i, j in pairs]


def swap(x, first):
    return lax.ppermute(x, ("clips", "rows"), neighbours(first))


def swap_both(for_even, for_odd):
    far = swap(for_odd, 1)
    near = swap(for_even, 0)
    return near, far


def halo_row(near_row, far_row, even, exists, upper):
    row = jnp.where(even, far_row, near_row) if upper else jnp.where(even, near_row, far_row)
    return jnp.where(exists, row, jnp.zeros_like(row))


def borders():
    mine = lax.axis_index("rows")
    return lax.rem(mine, 2) == 0, mine > 0, mine < lax.axis_size("rows") - 1


def tables_kernel(band, across, slots, row_hbm, col_hbm, feat_hbm, state_hbm,
                  table_ref, near_ref, far_ref, near_edge, far_edge, pool_ref, row_ref, col_ref, sem):
    frames, blocks = row_ref.shape
    rows = feat_hbm.shape[1]
    mine = lax.axis_index("rows")
    total = band * lax.axis_size("rows")
    even = lax.rem(mine, 2) == 0
    moves = [
        pltpu.make_async_copy(row_hbm, row_ref, sem.at[0]),
        pltpu.make_async_copy(col_hbm, col_ref, sem.at[1]),
    ]
    near_rows = pl.ds(jnp.where(even, rows - HALO, 0), HALO)
    far_rows = pl.ds(jnp.where(even, 0, rows - HALO), HALO)
    edges = [
        pltpu.make_async_copy(feat_hbm.at[0, near_rows], near_edge, sem.at[2]),
        pltpu.make_async_copy(feat_hbm.at[0, far_rows], far_edge, sem.at[3]),
    ]
    for copy in moves + edges:
        copy.start()
    for q in range(band):
        for r in range(BLK):
            pltpu.make_async_copy(
                state_hbm.at[q, r], pool_ref.at[pl.ds(q * across, across), r], sem.at[4]
            ).start()
    for copy in moves:
        copy.wait()
    block = lax.broadcasted_iota(jnp.int32, (frames, blocks), 1)
    source = jnp.clip(block // across + row_ref[...], -mine * band, total - 1 - mine * band)
    column = jnp.clip(block % across + col_ref[...], 0, across - 1)
    above = source < 0
    below = source >= band
    local = source * across + column + jnp.where(above, blocks, jnp.where(below, -blocks, 0))
    earlier = lax.broadcasted_iota(jnp.int32, (blocks, blocks), 0) < lax.broadcasted_iota(
        jnp.int32, (blocks, blocks), 1
    )
    earlier = jnp.where(earlier, 1.0, 0.0).astype(BF16)

    def rank(mask):
        ones = jnp.where(mask, 1.0, 0.0).astype(BF16)
        return jnp.dot(ones, earlier, preferred_element_type=F32).astype(jnp.int32)

    rank_above = rank(above)
    rank_below = rank(below)
    near_base = blocks
    far_base = blocks + slots
    above_base = jnp.where(even, far_base, near_base)
    below_base = jnp.where(even, near_base, far_base)
    table = jnp.where(above, above_base + rank_above, local)
    table_ref[...] = jnp.where(below, below_base + rank_below, table)
    near_rank = jnp.where(even, jnp.where(below, rank_below, -1), jnp.where(above, rank_above, -1))
    far_rank = jnp.where(even, jnp.where(above, rank_above, -1), jnp.where(below, rank_below, -1))
    length = near_ref.shape[1]
    slot = lax.broadcasted_iota(jnp.int32, (length, blocks), 0)
    for frame in range(frames):
        ids = local[frame:frame + 1].astype(F32).astype(BF16)
        for ranks, out in ((near_rank, near_ref), (far_rank, far_ref)):
            chosen = jnp.where(ranks[frame:frame + 1] == slot, 1.0, 0.0).astype(BF16)
            got = lax.dot_general(ids, chosen, (((1,), (1,)), ((), ())), preferred_element_type=F32)
            out[frame:frame + 1] = got.astype(jnp.int32)
    for copy in edges:
        copy.wait()
    pltpu.make_async_copy(pool_ref, pool_ref, sem.at[4]).wait()


def weights_kernel(merging_hbm, first_hbm, second_hbm, _,
                   feat_out, warp_out, first_out, second_out, merging_ref, first_ref, second_ref, sem):
    loads = [
        pltpu.make_async_copy(merging_hbm, merging_ref, sem.at[0]),
        pltpu.make_async_copy(first_hbm, first_ref, sem.at[1]),
        pltpu.make_async_copy(second_hbm, second_ref, sem.at[2]),
    ]
    for load in loads:
        load.start()
    chans = first_ref.shape[2]
    depth = 3 * chans
    for source, start, out, load in (
        (merging_ref, 0, feat_out, loads[0]),
        (merging_ref, chans, warp_out, None),
        (first_ref, 0, first_out, loads[1]),
        (second_ref, 0, second_out, loads[2]),
    ):
        if load is not None:
            load.wait()
        width = source.shape[3]
        zero = jnp.zeros((chans, width), BF16)
        for a in range(4):
            for e in range(3):
                top = a * depth + e * chans
                for half in range(2):
                    tap = a - half
                    if 0 <= tap < 3:
                        value = source[tap, e, start:start + chans, :]
                    else:
                        value = zero
                    out[top:top + chans, half * width:(half + 1) * width] = value


def pack(pool_ref, near_list, far_list, frame, near_out, far_out):
    for slot in range(near_out.shape[0]):
        near_out[slot] = pool_ref[near_list[frame, slot]]
        far_out[slot] = pool_ref[far_list[frame, slot]]


def pack_kernel(frame, pool_ref, near_list, far_list, near_out, far_out):
    pack(pool_ref, near_list, far_list, frame, near_out, far_out)


def shifter(pad_ref):
    slots, length, chans = pad_ref.shape
    cols = length - 2 * BLK
    edge = jnp.zeros((BLK, chans), F32)
    for slot in range(slots):
        pad_ref[slot, 0:BLK] = edge
        pad_ref[slot, BLK + cols:length] = edge
    turn = [0]

    def spread(out_ref, pair, half, value):
        slot = turn[0] % slots
        turn[0] += 1
        pad_ref[slot, BLK:BLK + cols] = value
        left = pad_ref[slot, BLK - 1:BLK - 1 + cols]
        right = pad_ref[slot, BLK + 1:BLK + 1 + cols]
        for e, part in enumerate((left, value, right)):
            out_ref[pair, half, :, e * chans:(e + 1) * chans] = part.astype(BF16)

    return spread


def pair_dot(x_ref, w_ref, pair, pairs):
    cols, depth = x_ref.shape[2:]
    parts = [
        x_ref[pair + a // 2:pair + a // 2 + pairs, a % 2].reshape(pairs * cols, depth)
        for a in range(4)
    ]
    return jnp.dot(jnp.concatenate(parts, axis=1), w_ref[...], preferred_element_type=F32)


def chunks(first, end, size):
    total = end - first
    count = -(-total // size)
    bounds = [first + total * n // count for n in range(count + 1)]
    return [(a, b - a) for a, b in zip(bounds, bounds[1:])]


def features_kernel(frame, feat_hbm, near_ref, far_ref, w_ref, out_ref, *refs):
    feat_ref, x_ref, pad_ref, sem, edge_sem = refs[-5:]
    rows, across, _, chans = feat_ref.shape
    cols = across * BLK
    even, has_above, has_below = borders()
    size = rows // sem.shape[0]
    spread = shifter(pad_ref)
    loads = []
    for n in range(sem.shape[0]):
        part = pl.ds(n * size, size)
        loads.append(pltpu.make_async_copy(feat_hbm.at[frame, part], feat_ref.at[part], sem.at[n]))
        loads[-1].start()
    starts = (jnp.where(even, rows - HALO, 0), jnp.where(even, 0, rows - HALO))
    for n, edge in enumerate(refs[:-5]):
        part = pl.ds(starts[n], HALO)
        loads.append(pltpu.make_async_copy(feat_hbm.at[frame + 1, part], edge, edge_sem.at[n]))
        loads[-1].start()
    for row in range(-HALO, rows + HALO):
        if row < 0:
            n = row + near_ref.shape[0]
            value = halo_row(near_ref[n], far_ref[n], even, has_above, True)
        elif row >= rows:
            n = row - rows + near_ref.shape[0] - HALO
            value = halo_row(near_ref[n], far_ref[n], even, has_below, False)
        else:
            if row % size == 0:
                loads[row // size].wait()
            value = feat_ref[row]
        value = value.astype(F32).reshape(cols, chans)
        spread(x_ref, (row + HALO) // 2, (row + HALO) % 2, value)
    for pair, pairs in chunks(0, rows // 2 + 2, STEP):
        out_ref[pair:pair + pairs] = pair_dot(x_ref, w_ref, pair, pairs).reshape(
            pairs, cols, out_ref.shape[2]
        )
    for load in loads[sem.shape[0]:]:
        load.wait()


def assemble_kernel(frame, table_ref, pool_ref, near_ref, far_ref, _, *refs):
    warped_out, near_edge, far_edge, all_ref = refs[-4:]
    rows, across = warped_out.shape[:2]
    blocks = pool_ref.shape[0]
    slots = near_ref.shape[0]
    odd = lax.rem(lax.axis_index("rows"), 2)
    near_rows = pl.ds(jnp.where(odd == 0, rows - HALO, 0), HALO)
    far_rows = pl.ds(jnp.where(odd == 0, 0, rows - HALO), HALO)
    for edge, feat_edge in zip((near_edge, far_edge), refs[:-4]):
        edge[HALO:2 * HALO] = feat_edge[...]
    all_ref[0:blocks] = pool_ref[...]
    all_ref[blocks:blocks + slots] = near_ref[...]
    all_ref[blocks + slots:blocks + 2 * slots] = far_ref[...]
    for block in range(blocks):
        q, p = divmod(block, across)
        warped_out[q * BLK:(q + 1) * BLK, p] = all_ref[table_ref[frame, block]]
    near_edge[0:HALO] = warped_out[near_rows]
    far_edge[0:HALO] = warped_out[far_rows]


def split_rows(value, pairs, cols, chans):
    for n in range(pairs):
        for half in range(2):
            yield n, half, value[n * cols:(n + 1) * cols, half * chans:(half + 1) * chans]


def finish(state_ref, pool_ref, centre, value, row, across, chans):
    done = (centre.astype(F32) + value).reshape(across, BLK, chans).astype(BF16)
    state_ref[row] = done
    if pool_ref is not None:
        q, r = divmod(row, BLK)
        pool_ref[q * across:(q + 1) * across, r] = done


def inner_kernel(frame, last, part_ref, warped_ref, w1_ref, w2_ref, w3_ref, *refs):
    if frame:
        refs = refs[1:]
    out_ref = refs[0]
    pool_ref = None if last else refs[1]
    m_edge, d_edge, x_ref, m_ref, d_ref, pad_ref, state_ref, sem = refs[-8:]
    spread = shifter(pad_ref)
    rows, across, _, chans = warped_ref.shape
    cols = across * BLK
    half_rows = rows // 2
    for row in range(rows):
        value = warped_ref[row].astype(F32).reshape(cols, chans)
        spread(x_ref, (row + HALO) // 2, (row + HALO) % 2, value)
    for pair, pairs in chunks(2, half_rows, STEP):
        raw = part_ref[pair:pair + pairs].reshape(pairs * cols, 2 * chans)
        raw = raw + pair_dot(x_ref, w1_ref, pair, pairs)
        value = jnp.maximum(raw, 0.1 * raw)
        for n, half, one in split_rows(value, pairs, cols, chans):
            spread(m_ref, pair + n, half, one)
    m_edge[0] = m_ref[2]
    m_edge[1] = m_ref[half_rows - 1]
    for pair, pairs in chunks(2, half_rows - 1, STEP):
        value = jnp.maximum(pair_dot(m_ref, w2_ref, pair, pairs), 0.0)
        for n, half, one in split_rows(value, pairs, cols, chans):
            spread(d_ref, pair + n, half, one)
    d_edge[0] = d_ref[2]
    d_edge[1] = d_ref[half_rows - 2]
    for pair, pairs in chunks(2, half_rows - 2, STEP):
        value = pair_dot(d_ref, w3_ref, pair, pairs)
        for n, half, one in split_rows(value, pairs, cols, chans):
            centre = m_ref[pair + n + 1, half, :, chans:2 * chans]
            finish(state_ref, pool_ref, centre, one, 2 * (pair + n) + half, across, chans)
        pltpu.make_async_copy(
            state_ref.at[pl.ds(2 * pair, 2 * pairs)],
            out_ref.at[frame, pl.ds(2 * pair, 2 * pairs)],
            sem,
        ).start()
    inner = pl.ds(4, rows - 8)
    pltpu.make_async_copy(state_ref.at[inner], out_ref.at[frame, inner], sem).wait()


def border_kernel(frame, last, part_ref, warped_ref, near_ref, far_ref, w1_ref, w2_ref, w3_ref,
                  m_edge, d_edge, *refs):
    if last:
        _, out_ref, x_ref, m_ref, d_ref, pad_ref, state_ref, sem = refs
        pool_ref = None
    else:
        _, _, near_list, far_list, out_ref, pool_ref, near_out, far_out = refs[:8]
        x_ref, m_ref, d_ref, pad_ref, state_ref, sem = refs[8:]
    spread = shifter(pad_ref)
    rows, across, _, chans = warped_ref.shape
    cols = across * BLK
    even, has_above, has_below = borders()
    depth = 3 * chans

    def edge_dot(ref, side, w_ref):
        parts = [ref[side, a // 2:a // 2 + 2, a % 2].reshape(2 * cols, depth) for a in range(4)]
        return jnp.dot(jnp.concatenate(parts, axis=1), w_ref[...], preferred_element_type=F32)

    def flat(value):
        return value.astype(F32).reshape(cols, chans)

    for n in range(HALO):
        above = halo_row(near_ref[n], far_ref[n], even, has_above, True)
        below = halo_row(near_ref[n], far_ref[n], even, has_below, False)
        spread(x_ref.at[0], n // 2, n % 2, flat(above))
        spread(x_ref.at[0], (n + 3) // 2, (n + 3) % 2, flat(warped_ref[n]))
        spread(x_ref.at[1], n // 2, n % 2, flat(warped_ref[rows - HALO + n]))
        spread(x_ref.at[1], (n + 3) // 2, (n + 3) % 2, flat(below))
    half_rows = rows // 2

    def masked(value, row):
        if row < 0:
            return jnp.where(has_above, value, 0.0)
        return jnp.where(has_below, value, 0.0) if row >= rows else value

    m_ref[0, 2] = m_edge[0]
    m_ref[1, 0] = m_edge[1]
    d_ref[0, 2] = d_edge[0]
    d_ref[1, 0] = d_edge[1]
    for side in range(2):
        first = side * half_rows
        raw = part_ref[first:first + 2].reshape(2 * cols, 2 * chans) + edge_dot(x_ref, side, w1_ref)
        value = jnp.maximum(raw, 0.1 * raw)
        for n, half, one in split_rows(value, 2, cols, chans):
            one = masked(one, 2 * (first + n) + half - 2)
            spread(m_ref.at[side], n + side, half, one)
    for side in range(2):
        first = side * (half_rows - 1)
        value = jnp.maximum(edge_dot(m_ref, side, w2_ref), 0.0)
        for n, half, one in split_rows(value, 2, cols, chans):
            one = masked(one, 2 * (first + n) + half - 1)
            spread(d_ref.at[side], n + side, half, one)
    for side in range(2):
        first = side * (half_rows - 2)
        value = edge_dot(d_ref, side, w3_ref)
        for n, half, one in split_rows(value, 2, cols, chans):
            centre = m_ref[side, n + 1 - side, half, :, chans:2 * chans]
            finish(state_ref, pool_ref, centre, one, 2 * (first + n) + half, across, chans)
    copies = []
    for n, start in enumerate((0, rows - 4)):
        part = pl.ds(start, 4)
        copies.append(pltpu.make_async_copy(state_ref.at[part], out_ref.at[frame, part], sem.at[n]))
        copies[-1].start()
    if not last:
        pack(pool_ref, near_list, far_list, frame + 1, near_out, far_out)
    for copy in copies:
        copy.wait()


def on_device(state_start, features, row_moves, col_moves, merging_weight, first_weight, second_weight):
    rows, cols, chans = state_start.shape
    frames = features.shape[0]
    band = rows // BLK
    across = cols // BLK
    blocks = band * across
    slots = blocks // 2
    list_len = slots + 8
    state = state_start.reshape(band, BLK, across, BLK, chans)
    feats = features.reshape(frames, rows, across, BLK, chans)
    block_shape = (BLK, BLK, chans)
    edge_shape = (HALO, across, BLK, chans)
    pool_shape = on_chip((blocks,) + block_shape)
    message = on_chip((slots,) + block_shape)

    table, near_list, far_list, near_feat, far_feat, pool = pl.pallas_call(
        functools.partial(tables_kernel, band, across, slots),
        out_shape=[
            on_chip((frames, blocks), jnp.int32),
            on_chip((frames, list_len), jnp.int32),
            on_chip((frames, list_len), jnp.int32),
            on_chip(edge_shape),
            on_chip(edge_shape),
            pool_shape,
        ],
        in_specs=[ANY] * 4,
        out_specs=[VMEM] * 6,
        scratch_shapes=[
            pltpu.VMEM((frames, blocks), jnp.int32),
            pltpu.VMEM((frames, blocks), jnp.int32),
            pltpu.SemaphoreType.DMA((5,)),
        ],
        compiler_params=room(4),
        name="tables",
    )(*map(in_hbm, (row_moves, col_moves, feats, state)))
    near_list, far_list = swap_both(near_list, far_list)
    near_feat, far_feat = swap_both(near_feat, far_feat)

    near_msg, far_msg = pl.pallas_call(
        functools.partial(pack_kernel, 0),
        out_shape=[message, message],
        in_specs=[VMEM, SMEM, SMEM],
        out_specs=[VMEM] * 2,
        compiler_params=room(4),
        name="pack",
    )(resident(pool), near_list, far_list)

    pair_shape = on_chip((4 * 3 * chans, 2 * chans))
    w_feat, w_warp, w_first, w_second = pl.pallas_call(
        weights_kernel,
        out_shape=[pair_shape] * 4,
        in_specs=[ANY] * 4,
        out_specs=[VMEM] * 4,
        scratch_shapes=[
            pltpu.VMEM(merging_weight.shape, BF16),
            pltpu.VMEM(first_weight.shape, BF16),
            pltpu.VMEM(second_weight.shape, BF16),
            pltpu.SemaphoreType.DMA((3,)),
        ],
        compiler_params=room(4),
        name="weights",
    )(*map(in_hbm, (merging_weight, first_weight, second_weight)), near_msg)

    pad_rows = pltpu.VMEM((8, cols + 2 * BLK, chans), F32)

    def wide(extra):
        return pltpu.VMEM((rows // 2 + extra, 2, cols, 3 * chans), BF16)

    def features_part(frame, near_feat, far_feat):
        passed = 0 if frame == frames - 1 else 2
        return pl.pallas_call(
            functools.partial(features_kernel, frame),
            out_shape=[on_chip((rows // 2 + 2, cols, 2 * chans), F32)] + [on_chip(edge_shape)] * passed,
            in_specs=[ANY] + [VMEM] * 3,
            out_specs=[VMEM] * (1 + passed),
            scratch_shapes=[
                pltpu.VMEM((rows, across, BLK, chans), BF16),
                wide(3),
                pad_rows,
                pltpu.SemaphoreType.DMA((4,)),
                pltpu.SemaphoreType.DMA((2,)),
            ],
            compiler_params=room(16),
            name="features",
        )(in_hbm(feats), resident(near_feat), resident(far_feat), resident(w_feat))

    out = None
    out_shape = shape_of((frames, rows, across, BLK, chans))
    edge_pairs = on_chip((2, 2, cols, 3 * chans))
    for frame in range(frames):
        last = frame == frames - 1
        near_got, far_got = swap_both(near_msg, far_msg)
        part, *next_edges = features_part(frame, near_feat, far_feat)
        sent_edge = on_chip(((1 if last else 2) * HALO,) + edge_shape[1:])
        warped, near_edge, far_edge = pl.pallas_call(
            functools.partial(assemble_kernel, frame),
            out_shape=[on_chip((rows, across, BLK, chans)), sent_edge, sent_edge],
            in_specs=[SMEM] + [VMEM] * 3 + [ANY] + [VMEM] * len(next_edges),
            out_specs=[VMEM] * 3,
            scratch_shapes=[pltpu.VMEM((blocks + 2 * slots,) + block_shape, BF16)],
            compiler_params=room(8),
            name="assemble",
        )(table, resident(pool), resident(near_got), resident(far_got), part, *map(resident, next_edges))
        near_halo, far_halo = swap_both(near_edge, far_edge)
        near_feat, far_feat = near_halo, far_halo
        args = tuple(map(resident, (part, warped, w_warp, w_first, w_second)))
        results = pl.pallas_call(
            functools.partial(inner_kernel, frame, last),
            out_shape=[out_shape] + [pool_shape] * (not last) + [edge_pairs] * 2,
            in_specs=[VMEM] * 5 + [ANY] * (frame > 0),
            out_specs=[ANY] + [VMEM] * (2 + (not last)),
            input_output_aliases={5: 0} if frame else {},
            scratch_shapes=[
                wide(3),
                wide(2),
                wide(1),
            pad_rows,
                pltpu.VMEM((rows, across, BLK, chans), BF16),
                pltpu.SemaphoreType.DMA,
            ],
            compiler_params=room(24),
            name="inner",
        )(*args, *([out] if frame else []))
        out = results[0]
        m_edge, d_edge = results[-2:]
        args = tuple(map(resident, (
            part, warped, near_halo, far_halo, w_warp, w_first, w_second, m_edge, d_edge
        )))
        scratch = [pltpu.VMEM((2, 3, 2, cols, 3 * chans), BF16) for _ in range(3)] + [
            pad_rows,
            pltpu.VMEM((rows, across, BLK, chans), BF16),
            pltpu.SemaphoreType.DMA((2,)),
        ]
        kernel = functools.partial(border_kernel, frame, last)
        if last:
            out = pl.pallas_call(
                kernel,
                out_shape=out_shape,
                in_specs=[VMEM] * 9 + [ANY],
                out_specs=ANY,
                input_output_aliases={9: 0},
                scratch_shapes=scratch,
                compiler_params=room(12),
                name="border",
            )(*args, out)
        else:
            out, pool, near_msg, far_msg = pl.pallas_call(
                kernel,
                out_shape=[out_shape, pool_shape, message, message],
                in_specs=[VMEM] * 9 + [ANY, VMEM] + [SMEM] * 2,
                out_specs=[ANY] + [VMEM] * 3,
                input_output_aliases={9: 0, 10: 1},
                scratch_shapes=scratch,
                compiler_params=room(12),
                name="border",
            )(*args, out, resident(results[1]), near_list, far_list)
    return out.reshape(frames, rows, cols, chans)


def solution(mesh):
    in_specs = (
        P(("clips", "rows"), None, None),
        P(None, ("clips", "rows"), None, None),
        P(None, ("clips", "rows")),
        P(None, ("clips", "rows")),
        P(),
        P(),
        P(),
    )
    out_specs = P(None, ("clips", "rows"), None, None)
    return jax.shard_map(
        on_device, mesh=mesh, in_specs=in_specs, out_specs=out_specs, check_vma=False
    )
```

```python
import functools

import jax
import jax.numpy as jnp
from jax import lax
from jax.experimental import pallas as pl
from jax.experimental.pallas import tpu as pltpu
from jax.sharding import PartitionSpec as P


BLK = 8
HALO = 3
STEP = 4
VMEM = pl.BlockSpec(memory_space=pltpu.VMEM)
SMEM = pl.BlockSpec(memory_space=pltpu.SMEM)
ANY = pl.BlockSpec(memory_space=pl.ANY)
BF16 = jnp.bfloat16
F32 = jnp.float32


def shape_of(shape, dtype=BF16):
    return jax.ShapeDtypeStruct(shape, dtype)


def on_chip(shape, dtype=BF16):
    return pltpu.VMEM(shape, dtype)


def room(mebibytes):
    return pltpu.CompilerParams(vmem_limit_bytes=mebibytes << 20)


def in_hbm(x):
    return pltpu.with_memory_space_constraint(x, pltpu.HBM)


def resident(x):
    return pltpu.with_memory_space_constraint(x, pltpu.VMEM)


def neighbours(first):
    clips, size = lax.axis_size("clips"), lax.axis_size("rows")
    inside = [(i, i + 1) for i in range(first, size - 1, 2)]
    pairs = [(c * size + i, c * size + j) for c in range(clips) for i, j in inside]
    left = [i for i in range(size) if not any(i in pair for pair in inside)]
    pairs += [(c * size + i, (c + 1) * size + i) for c in range(0, clips - 1, 2) for i in left]
    return pairs + [(j, i) for i, j in pairs]


def swap(x, first):
    return lax.ppermute(x, ("clips", "rows"), neighbours(first))


def swap_both(for_even, for_odd):
    far = swap(for_odd, 1)
    near = swap(for_even, 0)
    return near, far


def halo_row(near_row, far_row, even, exists, upper):
    row = jnp.where(even, far_row, near_row) if upper else jnp.where(even, near_row, far_row)
    return jnp.where(exists, row, jnp.zeros_like(row))


def borders():
    mine = lax.axis_index("rows")
    return lax.rem(mine, 2) == 0, mine > 0, mine < lax.axis_size("rows") - 1


def tables_kernel(band, across, slots, row_hbm, col_hbm, feat_hbm, state_hbm,
                  table_ref, near_ref, far_ref, near_edge, far_edge, pool_ref, row_ref, col_ref, sem):
    frames, blocks = row_ref.shape
    rows = feat_hbm.shape[1]
    mine = lax.axis_index("rows")
    total = band * lax.axis_size("rows")
    even = lax.rem(mine, 2) == 0
    moves = [
        pltpu.make_async_copy(row_hbm, row_ref, sem.at[0]),
        pltpu.make_async_copy(col_hbm, col_ref, sem.at[1]),
    ]
    near_rows = pl.ds(jnp.where(even, rows - HALO, 0), HALO)
    far_rows = pl.ds(jnp.where(even, 0, rows - HALO), HALO)
    edges = [
        pltpu.make_async_copy(feat_hbm.at[0, near_rows], near_edge, sem.at[2]),
        pltpu.make_async_copy(feat_hbm.at[0, far_rows], far_edge, sem.at[3]),
    ]
    for copy in moves + edges:
        copy.start()
    for q in range(band):
        for r in range(BLK):
            pltpu.make_async_copy(
                state_hbm.at[q, r], pool_ref.at[pl.ds(q * across, across), r], sem.at[4]
            ).start()
    for copy in moves:
        copy.wait()
    block = lax.broadcasted_iota(jnp.int32, (frames, blocks), 1)
    source = jnp.clip(block // across + row_ref[...], -mine * band, total - 1 - mine * band)
    column = jnp.clip(block % across + col_ref[...], 0, across - 1)
    above = source < 0
    below = source >= band
    local = source * across + column + jnp.where(above, blocks, jnp.where(below, -blocks, 0))
    earlier = lax.broadcasted_iota(jnp.int32, (blocks, blocks), 0) < lax.broadcasted_iota(
        jnp.int32, (blocks, blocks), 1
    )
    earlier = jnp.where(earlier, 1.0, 0.0).astype(BF16)

    def rank(mask):
        ones = jnp.where(mask, 1.0, 0.0).astype(BF16)
        return jnp.dot(ones, earlier, preferred_element_type=F32).astype(jnp.int32)

    rank_above = rank(above)
    rank_below = rank(below)
    near_base = blocks
    far_base = blocks + slots
    above_base = jnp.where(even, far_base, near_base)
    below_base = jnp.where(even, near_base, far_base)
    table = jnp.where(above, above_base + rank_above, local)
    table_ref[...] = jnp.where(below, below_base + rank_below, table)
    near_rank = jnp.where(even, jnp.where(below, rank_below, -1), jnp.where(above, rank_above, -1))
    far_rank = jnp.where(even, jnp.where(above, rank_above, -1), jnp.where(below, rank_below, -1))
    length = near_ref.shape[1]
    slot = lax.broadcasted_iota(jnp.int32, (length, blocks), 0)
    for frame in range(frames):
        ids = local[frame:frame + 1].astype(F32).astype(BF16)
        for ranks, out in ((near_rank, near_ref), (far_rank, far_ref)):
            chosen = jnp.where(ranks[frame:frame + 1] == slot, 1.0, 0.0).astype(BF16)
            got = lax.dot_general(ids, chosen, (((1,), (1,)), ((), ())), preferred_element_type=F32)
            out[frame:frame + 1] = got.astype(jnp.int32)
    for copy in edges:
        copy.wait()
    pltpu.make_async_copy(pool_ref, pool_ref, sem.at[4]).wait()


def weights_kernel(merging_hbm, first_hbm, second_hbm, _,
                   feat_out, warp_out, first_out, second_out, merging_ref, first_ref, second_ref, sem):
    loads = [
        pltpu.make_async_copy(merging_hbm, merging_ref, sem.at[0]),
        pltpu.make_async_copy(first_hbm, first_ref, sem.at[1]),
        pltpu.make_async_copy(second_hbm, second_ref, sem.at[2]),
    ]
    for load in loads:
        load.start()
    chans = first_ref.shape[2]
    depth = 3 * chans
    for source, start, out, load in (
        (merging_ref, 0, feat_out, loads[0]),
        (merging_ref, chans, warp_out, None),
        (first_ref, 0, first_out, loads[1]),
        (second_ref, 0, second_out, loads[2]),
    ):
        if load is not None:
            load.wait()
        width = source.shape[3]
        zero = jnp.zeros((chans, width), BF16)
        for a in range(4):
            for e in range(3):
                top = a * depth + e * chans
                for half in range(2):
                    tap = a - half
                    if 0 <= tap < 3:
                        value = source[tap, e, start:start + chans, :]
                    else:
                        value = zero
                    out[top:top + chans, half * width:(half + 1) * width] = value


def pack(pool_ref, near_list, far_list, frame, near_out, far_out):
    for slot in range(near_out.shape[0]):
        near_out[slot] = pool_ref[near_list[frame, slot]]
        far_out[slot] = pool_ref[far_list[frame, slot]]


def pack_kernel(frame, pool_ref, near_list, far_list, near_out, far_out):
    pack(pool_ref, near_list, far_list, frame, near_out, far_out)


def shifter(pad_ref):
    slots, length, chans = pad_ref.shape
    cols = length - 2 * BLK
    edge = jnp.zeros((BLK, chans), F32)
    for slot in range(slots):
        pad_ref[slot, 0:BLK] = edge
        pad_ref[slot, BLK + cols:length] = edge
    turn = [0]

    def spread(out_ref, pair, half, value):
        slot = turn[0] % slots
        turn[0] += 1
        pad_ref[slot, BLK:BLK + cols] = value
        left = pad_ref[slot, BLK - 1:BLK - 1 + cols]
        right = pad_ref[slot, BLK + 1:BLK + 1 + cols]
        for e, part in enumerate((left, value, right)):
            out_ref[pair, half, :, e * chans:(e + 1) * chans] = part.astype(BF16)

    return spread


def pair_dot(x_ref, w_ref, pair, pairs):
    cols, depth = x_ref.shape[2:]
    parts = [
        x_ref[pair + a // 2:pair + a // 2 + pairs, a % 2].reshape(pairs * cols, depth)
        for a in range(4)
    ]
    return jnp.dot(jnp.concatenate(parts, axis=1), w_ref[...], preferred_element_type=F32)


def chunks(first, end, size):
    total = end - first
    count = -(-total // size)
    bounds = [first + total * n // count for n in range(count + 1)]
    return [(a, b - a) for a, b in zip(bounds, bounds[1:])]


def features_kernel(frame, feat_hbm, near_ref, far_ref, w_ref, out_ref, *refs):
    feat_ref, x_ref, pad_ref, sem, edge_sem = refs[-5:]
    rows, across, _, chans = feat_ref.shape
    cols = across * BLK
    even, has_above, has_below = borders()
    size = rows // sem.shape[0]
    spread = shifter(pad_ref)
    loads = []
    for n in range(sem.shape[0]):
        part = pl.ds(n * size, size)
        loads.append(pltpu.make_async_copy(feat_hbm.at[frame, part], feat_ref.at[part], sem.at[n]))
        loads[-1].start()
    starts = (jnp.where(even, rows - HALO, 0), jnp.where(even, 0, rows - HALO))
    for n, edge in enumerate(refs[:-5]):
        part = pl.ds(starts[n], HALO)
        loads.append(pltpu.make_async_copy(feat_hbm.at[frame + 1, part], edge, edge_sem.at[n]))
        loads[-1].start()
    for row in range(-HALO, rows + HALO):
        if row < 0:
            n = row + near_ref.shape[0]
            value = halo_row(near_ref[n], far_ref[n], even, has_above, True)
        elif row >= rows:
            n = row - rows + near_ref.shape[0] - HALO
            value = halo_row(near_ref[n], far_ref[n], even, has_below, False)
        else:
            if row % size == 0:
                loads[row // size].wait()
            value = feat_ref[row]
        value = value.astype(F32).reshape(cols, chans)
        spread(x_ref, (row + HALO) // 2, (row + HALO) % 2, value)
    for pair, pairs in chunks(0, rows // 2 + 2, STEP):
        out_ref[pair:pair + pairs] = pair_dot(x_ref, w_ref, pair, pairs).reshape(
            pairs, cols, out_ref.shape[2]
        )
    for load in loads[sem.shape[0]:]:
        load.wait()


def assemble_kernel(frame, table_vmem, pool_ref, near_ref, far_ref, _, *refs):
    warped_out, near_edge, far_edge, all_ref, table_ref, table_sem = refs[-6:]
    table_copy = pltpu.make_async_copy(table_vmem, table_ref, table_sem)
    table_copy.start()
    rows, across = warped_out.shape[:2]
    blocks = pool_ref.shape[0]
    slots = near_ref.shape[0]
    odd = lax.rem(lax.axis_index("rows"), 2)
    near_rows = pl.ds(jnp.where(odd == 0, rows - HALO, 0), HALO)
    far_rows = pl.ds(jnp.where(odd == 0, 0, rows - HALO), HALO)
    for edge, feat_edge in zip((near_edge, far_edge), refs[:-6]):
        edge[HALO:2 * HALO] = feat_edge[...]
    all_ref[0:blocks] = pool_ref[...]
    all_ref[blocks:blocks + slots] = near_ref[...]
    all_ref[blocks + slots:blocks + 2 * slots] = far_ref[...]
    table_copy.wait()
    for block in range(blocks):
        q, p = divmod(block, across)
        warped_out[q * BLK:(q + 1) * BLK, p] = all_ref[table_ref[frame, block]]
    near_edge[0:HALO] = warped_out[near_rows]
    far_edge[0:HALO] = warped_out[far_rows]


def split_rows(value, pairs, cols, chans):
    for n in range(pairs):
        for half in range(2):
            yield n, half, value[n * cols:(n + 1) * cols, half * chans:(half + 1) * chans]


def finish(state_ref, pool_ref, centre, value, row, across, chans):
    done = (centre.astype(F32) + value).reshape(across, BLK, chans).astype(BF16)
    state_ref[row] = done
    if pool_ref is not None:
        q, r = divmod(row, BLK)
        pool_ref[q * across:(q + 1) * across, r] = done


def inner_kernel(frame, last, part_ref, warped_ref, w1_ref, w2_ref, w3_ref, *refs):
    if frame:
        refs = refs[1:]
    out_ref = refs[0]
    pool_ref = None if last else refs[1]
    m_edge, d_edge, x_ref, m_ref, d_ref, pad_ref, state_ref, sem = refs[-8:]
    spread = shifter(pad_ref)
    rows, across, _, chans = warped_ref.shape
    cols = across * BLK
    half_rows = rows // 2
    for row in range(rows):
        value = warped_ref[row].astype(F32).reshape(cols, chans)
        spread(x_ref, (row + HALO) // 2, (row + HALO) % 2, value)
    for pair, pairs in chunks(2, half_rows, STEP):
        raw = part_ref[pair:pair + pairs].reshape(pairs * cols, 2 * chans)
        raw = raw + pair_dot(x_ref, w1_ref, pair, pairs)
        value = jnp.maximum(raw, 0.1 * raw)
        for n, half, one in split_rows(value, pairs, cols, chans):
            spread(m_ref, pair + n, half, one)
    m_edge[0] = m_ref[2]
    m_edge[1] = m_ref[half_rows - 1]
    for pair, pairs in chunks(2, half_rows - 1, STEP):
        value = jnp.maximum(pair_dot(m_ref, w2_ref, pair, pairs), 0.0)
        for n, half, one in split_rows(value, pairs, cols, chans):
            spread(d_ref, pair + n, half, one)
    d_edge[0] = d_ref[2]
    d_edge[1] = d_ref[half_rows - 2]
    for pair, pairs in chunks(2, half_rows - 2, STEP):
        value = pair_dot(d_ref, w3_ref, pair, pairs)
        for n, half, one in split_rows(value, pairs, cols, chans):
            centre = m_ref[pair + n + 1, half, :, chans:2 * chans]
            finish(state_ref, pool_ref, centre, one, 2 * (pair + n) + half, across, chans)
        pltpu.make_async_copy(
            state_ref.at[pl.ds(2 * pair, 2 * pairs)],
            out_ref.at[frame, pl.ds(2 * pair, 2 * pairs)],
            sem,
        ).start()
    inner = pl.ds(4, rows - 8)
    pltpu.make_async_copy(state_ref.at[inner], out_ref.at[frame, inner], sem).wait()


def border_kernel(frame, last, part_ref, warped_ref, near_ref, far_ref, w1_ref, w2_ref, w3_ref,
                  m_edge, d_edge, *refs):
    if last:
        _, out_ref, x_ref, m_ref, d_ref, pad_ref, state_ref, sem = refs
        pool_ref = None
    else:
        _, _, near_vmem, far_vmem, out_ref, pool_ref, near_out, far_out = refs[:8]
        x_ref, m_ref, d_ref, pad_ref, state_ref, sem, near_list, far_list = refs[8:]
        lists = [
            pltpu.make_async_copy(near_vmem, near_list, sem.at[2]),
            pltpu.make_async_copy(far_vmem, far_list, sem.at[3]),
        ]
        for copy in lists:
            copy.start()
    spread = shifter(pad_ref)
    rows, across, _, chans = warped_ref.shape
    cols = across * BLK
    even, has_above, has_below = borders()
    depth = 3 * chans

    def edge_dot(ref, side, w_ref):
        parts = [ref[side, a // 2:a // 2 + 2, a % 2].reshape(2 * cols, depth) for a in range(4)]
        return jnp.dot(jnp.concatenate(parts, axis=1), w_ref[...], preferred_element_type=F32)

    def flat(value):
        return value.astype(F32).reshape(cols, chans)

    for n in range(HALO):
        above = halo_row(near_ref[n], far_ref[n], even, has_above, True)
        below = halo_row(near_ref[n], far_ref[n], even, has_below, False)
        spread(x_ref.at[0], n // 2, n % 2, flat(above))
        spread(x_ref.at[0], (n + 3) // 2, (n + 3) % 2, flat(warped_ref[n]))
        spread(x_ref.at[1], n // 2, n % 2, flat(warped_ref[rows - HALO + n]))
        spread(x_ref.at[1], (n + 3) // 2, (n + 3) % 2, flat(below))
    half_rows = rows // 2

    def masked(value, row):
        if row < 0:
            return jnp.where(has_above, value, 0.0)
        return jnp.where(has_below, value, 0.0) if row >= rows else value

    m_ref[0, 2] = m_edge[0]
    m_ref[1, 0] = m_edge[1]
    d_ref[0, 2] = d_edge[0]
    d_ref[1, 0] = d_edge[1]
    for side in range(2):
        first = side * half_rows
        raw = part_ref[first:first + 2].reshape(2 * cols, 2 * chans) + edge_dot(x_ref, side, w1_ref)
        value = jnp.maximum(raw, 0.1 * raw)
        for n, half, one in split_rows(value, 2, cols, chans):
            one = masked(one, 2 * (first + n) + half - 2)
            spread(m_ref.at[side], n + side, half, one)
    for side in range(2):
        first = side * (half_rows - 1)
        value = jnp.maximum(edge_dot(m_ref, side, w2_ref), 0.0)
        for n, half, one in split_rows(value, 2, cols, chans):
            one = masked(one, 2 * (first + n) + half - 1)
            spread(d_ref.at[side], n + side, half, one)
    copies = []
    for side in range(2):
        first = side * (half_rows - 2)
        value = edge_dot(d_ref, side, w3_ref)
        for n, half, one in split_rows(value, 2, cols, chans):
            centre = m_ref[side, n + 1 - side, half, :, chans:2 * chans]
            finish(state_ref, pool_ref, centre, one, 2 * (first + n) + half, across, chans)
        part = pl.ds(side * (rows - 4), 4)
        copies.append(pltpu.make_async_copy(state_ref.at[part], out_ref.at[frame, part], sem.at[side]))
        copies[-1].start()
    if not last:
        for copy in lists:
            copy.wait()
        pack(pool_ref, near_list, far_list, frame + 1, near_out, far_out)
    for copy in copies:
        copy.wait()


def on_device(state_start, features, row_moves, col_moves, merging_weight, first_weight, second_weight):
    rows, cols, chans = state_start.shape
    frames = features.shape[0]
    band = rows // BLK
    across = cols // BLK
    blocks = band * across
    slots = blocks // 2
    list_len = slots + 8
    state = state_start.reshape(band, BLK, across, BLK, chans)
    feats = features.reshape(frames, rows, across, BLK, chans)
    block_shape = (BLK, BLK, chans)
    edge_shape = (HALO, across, BLK, chans)
    pool_shape = on_chip((blocks,) + block_shape)
    message = on_chip((slots,) + block_shape)

    table, near_list, far_list, near_feat, far_feat, pool = pl.pallas_call(
        functools.partial(tables_kernel, band, across, slots),
        out_shape=[
            on_chip((frames, blocks), jnp.int32),
            on_chip((frames, list_len), jnp.int32),
            on_chip((frames, list_len), jnp.int32),
            on_chip(edge_shape),
            on_chip(edge_shape),
            pool_shape,
        ],
        in_specs=[ANY] * 4,
        out_specs=[VMEM] * 6,
        scratch_shapes=[
            pltpu.VMEM((frames, blocks), jnp.int32),
            pltpu.VMEM((frames, blocks), jnp.int32),
            pltpu.SemaphoreType.DMA((5,)),
        ],
        compiler_params=room(4),
        name="tables",
    )(*map(in_hbm, (row_moves, col_moves, feats, state)))
    near_list, far_list = swap_both(near_list, far_list)
    near_feat, far_feat = swap_both(near_feat, far_feat)

    near_msg, far_msg = pl.pallas_call(
        functools.partial(pack_kernel, 0),
        out_shape=[message, message],
        in_specs=[VMEM, SMEM, SMEM],
        out_specs=[VMEM] * 2,
        compiler_params=room(4),
        name="pack",
    )(resident(pool), near_list, far_list)

    pair_shape = on_chip((4 * 3 * chans, 2 * chans))
    w_feat, w_warp, w_first, w_second = pl.pallas_call(
        weights_kernel,
        out_shape=[pair_shape] * 4,
        in_specs=[ANY] * 4,
        out_specs=[VMEM] * 4,
        scratch_shapes=[
            pltpu.VMEM(merging_weight.shape, BF16),
            pltpu.VMEM(first_weight.shape, BF16),
            pltpu.VMEM(second_weight.shape, BF16),
            pltpu.SemaphoreType.DMA((3,)),
        ],
        compiler_params=room(4),
        name="weights",
    )(*map(in_hbm, (merging_weight, first_weight, second_weight)), near_msg)

    pad_rows = pltpu.VMEM((24, cols + 2 * BLK, chans), F32)

    def wide(extra):
        return pltpu.VMEM((rows // 2 + extra, 2, cols, 3 * chans), BF16)

    def features_part(frame, near_feat, far_feat):
        passed = 0 if frame == frames - 1 else 2
        return pl.pallas_call(
            functools.partial(features_kernel, frame),
            out_shape=[on_chip((rows // 2 + 2, cols, 2 * chans), F32)] + [on_chip(edge_shape)] * passed,
            in_specs=[ANY] + [VMEM] * 3,
            out_specs=[VMEM] * (1 + passed),
            scratch_shapes=[
                pltpu.VMEM((rows, across, BLK, chans), BF16),
                wide(3),
                pad_rows,
                pltpu.SemaphoreType.DMA((4,)),
                pltpu.SemaphoreType.DMA((2,)),
            ],
            compiler_params=room(16),
            name="features",
        )(in_hbm(feats), resident(near_feat), resident(far_feat), resident(w_feat))

    out = None
    out_shape = shape_of((frames, rows, across, BLK, chans))
    edge_pairs = on_chip((2, 2, cols, 3 * chans))
    for frame in range(frames):
        last = frame == frames - 1
        near_got, far_got = swap_both(near_msg, far_msg)
        part, *next_edges = features_part(frame, near_feat, far_feat)
        sent_edge = on_chip(((1 if last else 2) * HALO,) + edge_shape[1:])
        warped, near_edge, far_edge = pl.pallas_call(
            functools.partial(assemble_kernel, frame),
            out_shape=[on_chip((rows, across, BLK, chans)), sent_edge, sent_edge],
            in_specs=[VMEM] * 4 + [ANY] + [VMEM] * len(next_edges),
            out_specs=[VMEM] * 3,
            scratch_shapes=[
                pltpu.VMEM((blocks + 2 * slots,) + block_shape, BF16),
                pltpu.SMEM((frames, blocks), jnp.int32),
                pltpu.SemaphoreType.DMA,
            ],
            compiler_params=room(8),
            name="assemble",
        )(resident(table), resident(pool), resident(near_got), resident(far_got), part, *map(resident, next_edges))
        near_halo, far_halo = swap_both(near_edge, far_edge)
        near_feat, far_feat = near_halo, far_halo
        args = tuple(map(resident, (part, warped, w_warp, w_first, w_second)))
        results = pl.pallas_call(
            functools.partial(inner_kernel, frame, last),
            out_shape=[out_shape] + [pool_shape] * (not last) + [edge_pairs] * 2,
            in_specs=[VMEM] * 5 + [ANY] * (frame > 0),
            out_specs=[ANY] + [VMEM] * (2 + (not last)),
            input_output_aliases={5: 0} if frame else {},
            scratch_shapes=[
                wide(3),
                wide(2),
                wide(1),
            pad_rows,
                pltpu.VMEM((rows, across, BLK, chans), BF16),
                pltpu.SemaphoreType.DMA,
            ],
            compiler_params=room(24),
            name="inner",
        )(*args, *([out] if frame else []))
        out = results[0]
        m_edge, d_edge = results[-2:]
        args = tuple(map(resident, (
            part, warped, near_halo, far_halo, w_warp, w_first, w_second, m_edge, d_edge
        )))
        scratch = [pltpu.VMEM((2, 3, 2, cols, 3 * chans), BF16) for _ in range(3)] + [
            pad_rows,
            pltpu.VMEM((rows, across, BLK, chans), BF16),
            pltpu.SemaphoreType.DMA((4,)),
        ] + [pltpu.SMEM((frames, list_len), jnp.int32)] * (0 if last else 2)
        kernel = functools.partial(border_kernel, frame, last)
        if last:
            out = pl.pallas_call(
                kernel,
                out_shape=out_shape,
                in_specs=[VMEM] * 9 + [ANY],
                out_specs=ANY,
                input_output_aliases={9: 0},
                scratch_shapes=scratch,
                compiler_params=room(12),
                name="border",
            )(*args, out)
        else:
            out, pool, near_msg, far_msg = pl.pallas_call(
                kernel,
                out_shape=[out_shape, pool_shape, message, message],
                in_specs=[VMEM] * 9 + [ANY] + [VMEM] * 3,
                out_specs=[ANY] + [VMEM] * 3,
                input_output_aliases={9: 0, 10: 1},
                scratch_shapes=scratch,
                compiler_params=room(12),
                name="border",
            )(*args, out, resident(results[1]), resident(near_list), resident(far_list))
    return out.reshape(frames, rows, cols, chans)


def solution(mesh):
    in_specs = (
        P(("clips", "rows"), None, None),
        P(None, ("clips", "rows"), None, None),
        P(None, ("clips", "rows")),
        P(None, ("clips", "rows")),
        P(),
        P(),
        P(),
    )
    out_specs = P(None, ("clips", "rows"), None, None)
    return jax.shard_map(
        on_device, mesh=mesh, in_specs=in_specs, out_specs=out_specs, check_vma=False
    )
```

```python
import functools

import jax
import jax.numpy as jnp
from jax import lax
from jax.experimental import pallas as pl
from jax.experimental.pallas import tpu as pltpu
from jax.sharding import PartitionSpec as P


BLK = 8
HALO = 3
STEP = 4
VMEM = pl.BlockSpec(memory_space=pltpu.VMEM)
SMEM = pl.BlockSpec(memory_space=pltpu.SMEM)
ANY = pl.BlockSpec(memory_space=pl.ANY)
BF16 = jnp.bfloat16
F32 = jnp.float32


def shape_of(shape, dtype=BF16):
    return jax.ShapeDtypeStruct(shape, dtype)


def on_chip(shape, dtype=BF16):
    return pltpu.VMEM(shape, dtype)


def room(mebibytes):
    return pltpu.CompilerParams(vmem_limit_bytes=mebibytes << 20)


def in_hbm(x):
    return pltpu.with_memory_space_constraint(x, pltpu.HBM)


def resident(x):
    return pltpu.with_memory_space_constraint(x, pltpu.VMEM)


def neighbours(first):
    clips, size = lax.axis_size("clips"), lax.axis_size("rows")
    inside = [(i, i + 1) for i in range(first, size - 1, 2)]
    pairs = [(c * size + i, c * size + j) for c in range(clips) for i, j in inside]
    left = [i for i in range(size) if not any(i in pair for pair in inside)]
    pairs += [(c * size + i, (c + 1) * size + i) for c in range(0, clips - 1, 2) for i in left]
    return pairs + [(j, i) for i, j in pairs]


def swap(x, first):
    return lax.ppermute(x, ("clips", "rows"), neighbours(first))


def swap_both(for_even, for_odd):
    far = swap(for_odd, 1)
    near = swap(for_even, 0)
    return near, far


def halo_row(near_row, far_row, even, exists, upper):
    row = jnp.where(even, far_row, near_row) if upper else jnp.where(even, near_row, far_row)
    return jnp.where(exists, row, jnp.zeros_like(row))


def borders():
    mine = lax.axis_index("rows")
    return lax.rem(mine, 2) == 0, mine > 0, mine < lax.axis_size("rows") - 1


def tables_kernel(band, across, slots, row_hbm, col_hbm, feat_hbm, state_hbm,
                  table_ref, near_ref, far_ref, near_edge, far_edge, pool_ref, row_ref, col_ref, sem):
    frames, blocks = row_ref.shape
    rows = feat_hbm.shape[1]
    mine = lax.axis_index("rows")
    total = band * lax.axis_size("rows")
    even = lax.rem(mine, 2) == 0
    moves = [
        pltpu.make_async_copy(row_hbm, row_ref, sem.at[0]),
        pltpu.make_async_copy(col_hbm, col_ref, sem.at[1]),
    ]
    near_rows = pl.ds(jnp.where(even, rows - HALO, 0), HALO)
    far_rows = pl.ds(jnp.where(even, 0, rows - HALO), HALO)
    edges = [
        pltpu.make_async_copy(feat_hbm.at[0, near_rows], near_edge, sem.at[2]),
        pltpu.make_async_copy(feat_hbm.at[0, far_rows], far_edge, sem.at[3]),
    ]
    for copy in moves + edges:
        copy.start()
    for q in range(band):
        for r in range(BLK):
            pltpu.make_async_copy(
                state_hbm.at[q, r], pool_ref.at[pl.ds(q * across, across), r], sem.at[4]
            ).start()
    for copy in moves:
        copy.wait()
    block = lax.broadcasted_iota(jnp.int32, (frames, blocks), 1)
    source = jnp.clip(block // across + row_ref[...], -mine * band, total - 1 - mine * band)
    column = jnp.clip(block % across + col_ref[...], 0, across - 1)
    above = source < 0
    below = source >= band
    local = source * across + column + jnp.where(above, blocks, jnp.where(below, -blocks, 0))
    earlier = lax.broadcasted_iota(jnp.int32, (blocks, blocks), 0) < lax.broadcasted_iota(
        jnp.int32, (blocks, blocks), 1
    )
    earlier = jnp.where(earlier, 1.0, 0.0).astype(BF16)

    def rank(mask):
        ones = jnp.where(mask, 1.0, 0.0).astype(BF16)
        return jnp.dot(ones, earlier, preferred_element_type=F32).astype(jnp.int32)

    rank_above = rank(above)
    rank_below = rank(below)
    near_base = blocks
    far_base = blocks + slots
    above_base = jnp.where(even, far_base, near_base)
    below_base = jnp.where(even, near_base, far_base)
    table = jnp.where(above, above_base + rank_above, local)
    table_ref[...] = jnp.where(below, below_base + rank_below, table)
    near_rank = jnp.where(even, jnp.where(below, rank_below, -1), jnp.where(above, rank_above, -1))
    far_rank = jnp.where(even, jnp.where(above, rank_above, -1), jnp.where(below, rank_below, -1))
    length = near_ref.shape[1]
    slot = lax.broadcasted_iota(jnp.int32, (length, blocks), 0)
    for frame in range(frames):
        ids = local[frame:frame + 1].astype(F32).astype(BF16)
        for ranks, out in ((near_rank, near_ref), (far_rank, far_ref)):
            chosen = jnp.where(ranks[frame:frame + 1] == slot, 1.0, 0.0).astype(BF16)
            got = lax.dot_general(ids, chosen, (((1,), (1,)), ((), ())), preferred_element_type=F32)
            out[frame:frame + 1] = got.astype(jnp.int32)
    for copy in edges:
        copy.wait()
    pltpu.make_async_copy(pool_ref, pool_ref, sem.at[4]).wait()


def weights_kernel(merging_hbm, first_hbm, second_hbm, _,
                   feat_out, warp_out, first_out, second_out, merging_ref, first_ref, second_ref, sem):
    loads = [
        pltpu.make_async_copy(merging_hbm, merging_ref, sem.at[0]),
        pltpu.make_async_copy(first_hbm, first_ref, sem.at[1]),
        pltpu.make_async_copy(second_hbm, second_ref, sem.at[2]),
    ]
    for load in loads:
        load.start()
    chans = first_ref.shape[2]
    depth = 3 * chans
    for source, start, out, load in (
        (merging_ref, 0, feat_out, loads[0]),
        (merging_ref, chans, warp_out, None),
        (first_ref, 0, first_out, loads[1]),
        (second_ref, 0, second_out, loads[2]),
    ):
        if load is not None:
            load.wait()
        width = source.shape[3]
        zero = jnp.zeros((chans, width), BF16)
        for a in range(4):
            for e in range(3):
                top = a * depth + e * chans
                for half in range(2):
                    tap = a - half
                    if 0 <= tap < 3:
                        value = source[tap, e, start:start + chans, :]
                    else:
                        value = zero
                    out[top:top + chans, half * width:(half + 1) * width] = value


def pack(pool_ref, near_list, far_list, frame, near_out, far_out):
    for slot in range(near_out.shape[0]):
        near_out[slot] = pool_ref[near_list[frame, slot]]
        far_out[slot] = pool_ref[far_list[frame, slot]]


def pack_kernel(frame, pool_ref, near_list, far_list, near_out, far_out):
    pack(pool_ref, near_list, far_list, frame, near_out, far_out)


def shifter(pad_ref):
    slots, length, chans = pad_ref.shape
    cols = length - 2 * BLK
    edge = jnp.zeros((BLK, chans), F32)
    for slot in range(slots):
        pad_ref[slot, 0:BLK] = edge
        pad_ref[slot, BLK + cols:length] = edge
    turn = [0]

    def spread(out_ref, pair, half, value):
        slot = turn[0] % slots
        turn[0] += 1
        pad_ref[slot, BLK:BLK + cols] = value
        left = pad_ref[slot, BLK - 1:BLK - 1 + cols]
        right = pad_ref[slot, BLK + 1:BLK + 1 + cols]
        for e, part in enumerate((left, value, right)):
            out_ref[pair, half, :, e * chans:(e + 1) * chans] = part.astype(BF16)

    return spread


def pair_dot(x_ref, w_ref, pair, pairs):
    cols, depth = x_ref.shape[2:]
    parts = [
        x_ref[pair + a // 2:pair + a // 2 + pairs, a % 2].reshape(pairs * cols, depth)
        for a in range(4)
    ]
    return jnp.dot(jnp.concatenate(parts, axis=1), w_ref[...], preferred_element_type=F32)


def chunks(first, end, size):
    total = end - first
    count = -(-total // size)
    bounds = [first + total * n // count for n in range(count + 1)]
    return [(a, b - a) for a, b in zip(bounds, bounds[1:])]


def features_kernel(frame, passed, feat_hbm, near_ref, far_ref, w_ref, *refs):
    feat_ref, x_ref, pad_ref, sem, edge_sem = refs[-5:]
    outs = refs[min(frame, 2):-5]
    out_ref, edges = outs[0], outs[1:1 + passed]
    rows, across, _, chans = feat_ref.shape
    cols = across * BLK
    even, has_above, has_below = borders()
    size = rows // sem.shape[0]
    spread = shifter(pad_ref)
    loads = []
    for n in range(sem.shape[0]):
        part = pl.ds(n * size, size)
        loads.append(pltpu.make_async_copy(feat_hbm.at[frame, part], feat_ref.at[part], sem.at[n]))
        loads[-1].start()
    starts = (jnp.where(even, rows - HALO, 0), jnp.where(even, 0, rows - HALO))
    for n, edge in enumerate(edges):
        part = pl.ds(starts[n], HALO)
        loads.append(pltpu.make_async_copy(feat_hbm.at[frame + 1, part], edge, edge_sem.at[n]))
        loads[-1].start()
    if frame:
        loads.append(pltpu.make_async_copy(refs[0], outs[-1].at[frame - 1], edge_sem.at[2]))
        loads[-1].start()
    for row in range(-HALO, rows + HALO):
        if row < 0:
            n = row + near_ref.shape[0]
            value = halo_row(near_ref[n], far_ref[n], even, has_above, True)
        elif row >= rows:
            n = row - rows + near_ref.shape[0] - HALO
            value = halo_row(near_ref[n], far_ref[n], even, has_below, False)
        else:
            if row % size == 0:
                loads[row // size].wait()
            value = feat_ref[row]
        value = value.astype(F32).reshape(cols, chans)
        spread(x_ref, (row + HALO) // 2, (row + HALO) % 2, value)
    for pair, pairs in chunks(0, rows // 2 + 2, STEP):
        out_ref[pair:pair + pairs] = pair_dot(x_ref, w_ref, pair, pairs).reshape(
            pairs, cols, out_ref.shape[2]
        )
    for load in loads[sem.shape[0]:]:
        load.wait()


def assemble_kernel(frame, table_vmem, pool_ref, near_ref, far_ref, _, *refs):
    warped_out, near_edge, far_edge, all_ref, table_ref, table_sem = refs[-6:]
    table_copy = pltpu.make_async_copy(table_vmem, table_ref, table_sem)
    table_copy.start()
    rows, across = warped_out.shape[:2]
    blocks = pool_ref.shape[0]
    slots = near_ref.shape[0]
    odd = lax.rem(lax.axis_index("rows"), 2)
    near_rows = pl.ds(jnp.where(odd == 0, rows - HALO, 0), HALO)
    far_rows = pl.ds(jnp.where(odd == 0, 0, rows - HALO), HALO)
    for edge, feat_edge in zip((near_edge, far_edge), refs[:-6]):
        edge[HALO:2 * HALO] = feat_edge[...]
    all_ref[0:blocks] = pool_ref[...]
    all_ref[blocks:blocks + slots] = near_ref[...]
    all_ref[blocks + slots:blocks + 2 * slots] = far_ref[...]
    table_copy.wait()
    for block in range(blocks):
        q, p = divmod(block, across)
        warped_out[q * BLK:(q + 1) * BLK, p] = all_ref[table_ref[frame, block]]
    near_edge[0:HALO] = warped_out[near_rows]
    far_edge[0:HALO] = warped_out[far_rows]


def split_rows(value, pairs, cols, chans):
    for n in range(pairs):
        for half in range(2):
            yield n, half, value[n * cols:(n + 1) * cols, half * chans:(half + 1) * chans]


def finish(state_ref, pool_ref, centre, value, row, across, chans):
    done = (centre.astype(F32) + value).reshape(across, BLK, chans).astype(BF16)
    state_ref[row] = done
    if pool_ref is not None:
        q, r = divmod(row, BLK)
        pool_ref[q * across:(q + 1) * across, r] = done


def inner_kernel(last, part_ref, warped_ref, w1_ref, w2_ref, w3_ref, state_ref, *refs):
    pool_ref = None if last else refs[0]
    m_edge, d_edge, x_ref, m_ref, d_ref, pad_ref = refs[-6:]
    spread = shifter(pad_ref)
    rows, across, _, chans = warped_ref.shape
    cols = across * BLK
    half_rows = rows // 2
    for row in range(rows):
        value = warped_ref[row].astype(F32).reshape(cols, chans)
        spread(x_ref, (row + HALO) // 2, (row + HALO) % 2, value)
    for pair, pairs in chunks(2, half_rows, STEP):
        raw = part_ref[pair:pair + pairs].reshape(pairs * cols, 2 * chans)
        raw = raw + pair_dot(x_ref, w1_ref, pair, pairs)
        value = jnp.maximum(raw, 0.1 * raw)
        for n, half, one in split_rows(value, pairs, cols, chans):
            spread(m_ref, pair + n, half, one)
    m_edge[0] = m_ref[2]
    m_edge[1] = m_ref[half_rows - 1]
    for pair, pairs in chunks(2, half_rows - 1, STEP):
        value = jnp.maximum(pair_dot(m_ref, w2_ref, pair, pairs), 0.0)
        for n, half, one in split_rows(value, pairs, cols, chans):
            spread(d_ref, pair + n, half, one)
    d_edge[0] = d_ref[2]
    d_edge[1] = d_ref[half_rows - 2]
    for pair, pairs in chunks(2, half_rows - 2, STEP):
        value = pair_dot(d_ref, w3_ref, pair, pairs)
        for n, half, one in split_rows(value, pairs, cols, chans):
            centre = m_ref[pair + n + 1, half, :, chans:2 * chans]
            finish(state_ref, pool_ref, centre, one, 2 * (pair + n) + half, across, chans)


def border_kernel(frame, last, part_ref, warped_ref, near_ref, far_ref, w1_ref, w2_ref, w3_ref,
                  m_edge, d_edge, *refs):
    if last:
        state_in, _, out_ref, x_ref, m_ref, d_ref, pad_ref, sem, state_ref = refs
        pool_ref = None
        inner = pl.ds(4, warped_ref.shape[0] - 8)
        copies = [pltpu.make_async_copy(state_in.at[inner], out_ref.at[frame, inner], sem.at[2])]
        copies[0].start()
    else:
        _, _, near_vmem, far_vmem, state_ref, pool_ref, near_out, far_out = refs[:8]
        x_ref, m_ref, d_ref, pad_ref, sem, near_list, far_list = refs[8:]
        lists = [
            pltpu.make_async_copy(near_vmem, near_list, sem.at[2]),
            pltpu.make_async_copy(far_vmem, far_list, sem.at[3]),
        ]
        for copy in lists:
            copy.start()
    spread = shifter(pad_ref)
    rows, across, _, chans = warped_ref.shape
    cols = across * BLK
    even, has_above, has_below = borders()
    depth = 3 * chans

    def edge_dot(ref, side, w_ref):
        parts = [ref[side, a // 2:a // 2 + 2, a % 2].reshape(2 * cols, depth) for a in range(4)]
        return jnp.dot(jnp.concatenate(parts, axis=1), w_ref[...], preferred_element_type=F32)

    def flat(value):
        return value.astype(F32).reshape(cols, chans)

    for n in range(HALO):
        above = halo_row(near_ref[n], far_ref[n], even, has_above, True)
        below = halo_row(near_ref[n], far_ref[n], even, has_below, False)
        spread(x_ref.at[0], n // 2, n % 2, flat(above))
        spread(x_ref.at[0], (n + 3) // 2, (n + 3) % 2, flat(warped_ref[n]))
        spread(x_ref.at[1], n // 2, n % 2, flat(warped_ref[rows - HALO + n]))
        spread(x_ref.at[1], (n + 3) // 2, (n + 3) % 2, flat(below))
    half_rows = rows // 2

    def masked(value, row):
        if row < 0:
            return jnp.where(has_above, value, 0.0)
        return jnp.where(has_below, value, 0.0) if row >= rows else value

    m_ref[0, 2] = m_edge[0]
    m_ref[1, 0] = m_edge[1]
    d_ref[0, 2] = d_edge[0]
    d_ref[1, 0] = d_edge[1]
    for side in range(2):
        first = side * half_rows
        raw = part_ref[first:first + 2].reshape(2 * cols, 2 * chans) + edge_dot(x_ref, side, w1_ref)
        value = jnp.maximum(raw, 0.1 * raw)
        for n, half, one in split_rows(value, 2, cols, chans):
            one = masked(one, 2 * (first + n) + half - 2)
            spread(m_ref.at[side], n + side, half, one)
    for side in range(2):
        first = side * (half_rows - 1)
        value = jnp.maximum(edge_dot(m_ref, side, w2_ref), 0.0)
        for n, half, one in split_rows(value, 2, cols, chans):
            one = masked(one, 2 * (first + n) + half - 1)
            spread(d_ref.at[side], n + side, half, one)
    for side in range(2):
        first = side * (half_rows - 2)
        value = edge_dot(d_ref, side, w3_ref)
        for n, half, one in split_rows(value, 2, cols, chans):
            centre = m_ref[side, n + 1 - side, half, :, chans:2 * chans]
            finish(state_ref, pool_ref, centre, one, 2 * (first + n) + half, across, chans)
        if last:
            part = pl.ds(side * (rows - 4), 4)
            copies.append(pltpu.make_async_copy(state_ref.at[part], out_ref.at[frame, part], sem.at[side]))
            copies[-1].start()
    if last:
        for copy in copies:
            copy.wait()
    else:
        for copy in lists:
            copy.wait()
        pack(pool_ref, near_list, far_list, frame + 1, near_out, far_out)


def on_device(state_start, features, row_moves, col_moves, merging_weight, first_weight, second_weight):
    rows, cols, chans = state_start.shape
    frames = features.shape[0]
    band = rows // BLK
    across = cols // BLK
    blocks = band * across
    slots = blocks // 2
    list_len = slots + 8
    state = state_start.reshape(band, BLK, across, BLK, chans)
    feats = features.reshape(frames, rows, across, BLK, chans)
    block_shape = (BLK, BLK, chans)
    edge_shape = (HALO, across, BLK, chans)
    pool_shape = on_chip((blocks,) + block_shape)
    message = on_chip((slots,) + block_shape)

    table, near_list, far_list, near_feat, far_feat, pool = pl.pallas_call(
        functools.partial(tables_kernel, band, across, slots),
        out_shape=[
            on_chip((frames, blocks), jnp.int32),
            on_chip((frames, list_len), jnp.int32),
            on_chip((frames, list_len), jnp.int32),
            on_chip(edge_shape),
            on_chip(edge_shape),
            pool_shape,
        ],
        in_specs=[ANY] * 4,
        out_specs=[VMEM] * 6,
        scratch_shapes=[
            pltpu.VMEM((frames, blocks), jnp.int32),
            pltpu.VMEM((frames, blocks), jnp.int32),
            pltpu.SemaphoreType.DMA((5,)),
        ],
        compiler_params=room(4),
        name="tables",
    )(*map(in_hbm, (row_moves, col_moves, feats, state)))
    near_list, far_list = swap_both(near_list, far_list)
    near_feat, far_feat = swap_both(near_feat, far_feat)

    near_msg, far_msg = pl.pallas_call(
        functools.partial(pack_kernel, 0),
        out_shape=[message, message],
        in_specs=[VMEM, SMEM, SMEM],
        out_specs=[VMEM] * 2,
        compiler_params=room(4),
        name="pack",
    )(resident(pool), near_list, far_list)

    pair_shape = on_chip((4 * 3 * chans, 2 * chans))
    w_feat, w_warp, w_first, w_second = pl.pallas_call(
        weights_kernel,
        out_shape=[pair_shape] * 4,
        in_specs=[ANY] * 4,
        out_specs=[VMEM] * 4,
        scratch_shapes=[
            pltpu.VMEM(merging_weight.shape, BF16),
            pltpu.VMEM(first_weight.shape, BF16),
            pltpu.VMEM(second_weight.shape, BF16),
            pltpu.SemaphoreType.DMA((3,)),
        ],
        compiler_params=room(4),
        name="weights",
    )(*map(in_hbm, (merging_weight, first_weight, second_weight)), near_msg)

    pad_rows = pltpu.VMEM((24, cols + 2 * BLK, chans), F32)

    def wide(extra):
        return pltpu.VMEM((rows // 2 + extra, 2, cols, 3 * chans), BF16)

    out_shape = shape_of((frames, rows, across, BLK, chans))

    def features_part(frame, near_feat, far_feat, before, out):
        passed = 0 if frame == frames - 1 else 2
        done = ([resident(before)] if frame else []) + ([out] if frame > 1 else [])
        return pl.pallas_call(
            functools.partial(features_kernel, frame, passed),
            out_shape=[on_chip((rows // 2 + 2, cols, 2 * chans), F32)]
            + [on_chip(edge_shape)] * passed
            + [out_shape] * (frame > 0),
            in_specs=[ANY] + [VMEM] * 3 + [VMEM] * (frame > 0) + [ANY] * (frame > 1),
            out_specs=[VMEM] * (1 + passed) + [ANY] * (frame > 0),
            input_output_aliases={5: 1 + passed} if frame > 1 else {},
            scratch_shapes=[
                pltpu.VMEM((rows, across, BLK, chans), BF16),
                wide(3),
                pad_rows,
                pltpu.SemaphoreType.DMA((4,)),
                pltpu.SemaphoreType.DMA((3,)),
            ],
            compiler_params=room(16),
            name="features",
        )(in_hbm(feats), resident(near_feat), resident(far_feat), resident(w_feat), *done)

    out = state_now = None
    state_shape = on_chip((rows, across, BLK, chans))
    edge_pairs = on_chip((2, 2, cols, 3 * chans))
    for frame in range(frames):
        last = frame == frames - 1
        near_got, far_got = swap_both(near_msg, far_msg)
        part, *next_edges = features_part(frame, near_feat, far_feat, state_now, out)
        if frame:
            out = next_edges.pop()
        sent_edge = on_chip(((1 if last else 2) * HALO,) + edge_shape[1:])
        warped, near_edge, far_edge = pl.pallas_call(
            functools.partial(assemble_kernel, frame),
            out_shape=[on_chip((rows, across, BLK, chans)), sent_edge, sent_edge],
            in_specs=[VMEM] * 4 + [ANY] + [VMEM] * len(next_edges),
            out_specs=[VMEM] * 3,
            scratch_shapes=[
                pltpu.VMEM((blocks + 2 * slots,) + block_shape, BF16),
                pltpu.SMEM((frames, blocks), jnp.int32),
                pltpu.SemaphoreType.DMA,
            ],
            compiler_params=room(8),
            name="assemble",
        )(resident(table), resident(pool), resident(near_got), resident(far_got), part, *map(resident, next_edges))
        near_halo, far_halo = swap_both(near_edge, far_edge)
        near_feat, far_feat = near_halo, far_halo
        args = tuple(map(resident, (part, warped, w_warp, w_first, w_second)))
        state_now, *results = pl.pallas_call(
            functools.partial(inner_kernel, last),
            out_shape=[state_shape] + [pool_shape] * (not last) + [edge_pairs] * 2,
            in_specs=[VMEM] * 5,
            out_specs=[VMEM] * (3 + (not last)),
            scratch_shapes=[wide(3), wide(2), wide(1), pad_rows],
            compiler_params=room(24),
            name="inner",
        )(*args)
        m_edge, d_edge = results[-2:]
        args = tuple(map(resident, (
            part, warped, near_halo, far_halo, w_warp, w_first, w_second, m_edge, d_edge
        )))
        scratch = [pltpu.VMEM((2, 3, 2, cols, 3 * chans), BF16) for _ in range(3)] + [
            pad_rows,
            pltpu.SemaphoreType.DMA((4,)),
        ]
        if last:
            scratch.append(pltpu.VMEM((rows, across, BLK, chans), BF16))
        else:
            scratch += [pltpu.SMEM((frames, list_len), jnp.int32)] * 2
        kernel = functools.partial(border_kernel, frame, last)
        if last:
            out = pl.pallas_call(
                kernel,
                out_shape=out_shape,
                in_specs=[VMEM] * 10 + [ANY],
                out_specs=ANY,
                input_output_aliases={10: 0},
                scratch_shapes=scratch,
                compiler_params=room(12),
                name="border",
            )(*args, resident(state_now), out)
        else:
            state_now, pool, near_msg, far_msg = pl.pallas_call(
                kernel,
                out_shape=[state_shape, pool_shape, message, message],
                in_specs=[VMEM] * 13,
                out_specs=[VMEM] * 4,
                input_output_aliases={9: 0, 10: 1},
                scratch_shapes=scratch,
                compiler_params=room(12),
                name="border",
            )(*args, *map(resident, (state_now, results[0], near_list, far_list)))
    return out.reshape(frames, rows, cols, chans)


def solution(mesh):
    in_specs = (
        P(("clips", "rows"), None, None),
        P(None, ("clips", "rows"), None, None),
        P(None, ("clips", "rows")),
        P(None, ("clips", "rows")),
        P(),
        P(),
        P(),
    )
    out_specs = P(None, ("clips", "rows"), None, None)
    return jax.shard_map(
        on_device, mesh=mesh, in_specs=in_specs, out_specs=out_specs, check_vma=False
    )
```

```python
import functools

import jax
import jax.numpy as jnp
from jax import lax
from jax.experimental import pallas as pl
from jax.experimental.pallas import tpu as pltpu
from jax.sharding import PartitionSpec as P


BLK = 8
HALO = 3
STEP = 4
VMEM = pl.BlockSpec(memory_space=pltpu.VMEM)
SMEM = pl.BlockSpec(memory_space=pltpu.SMEM)
ANY = pl.BlockSpec(memory_space=pl.ANY)
BF16 = jnp.bfloat16
F32 = jnp.float32


def shape_of(shape, dtype=BF16):
    return jax.ShapeDtypeStruct(shape, dtype)


def on_chip(shape, dtype=BF16):
    return pltpu.VMEM(shape, dtype)


def room(mebibytes):
    return pltpu.CompilerParams(vmem_limit_bytes=mebibytes << 20)


def in_hbm(x):
    return pltpu.with_memory_space_constraint(x, pltpu.HBM)


def resident(x):
    return pltpu.with_memory_space_constraint(x, pltpu.VMEM)


def neighbours(first):
    clips, size = lax.axis_size("clips"), lax.axis_size("rows")
    inside = [(i, i + 1) for i in range(first, size - 1, 2)]
    pairs = [(c * size + i, c * size + j) for c in range(clips) for i, j in inside]
    left = [i for i in range(size) if not any(i in pair for pair in inside)]
    pairs += [(c * size + i, (c + 1) * size + i) for c in range(0, clips - 1, 2) for i in left]
    return pairs + [(j, i) for i, j in pairs]


def swap(x, first):
    return lax.ppermute(x, ("clips", "rows"), neighbours(first))


def swap_both(for_even, for_odd):
    far = swap(for_odd, 1)
    near = swap(for_even, 0)
    return near, far


def halo_row(near_row, far_row, even, exists, upper):
    row = jnp.where(even, far_row, near_row) if upper else jnp.where(even, near_row, far_row)
    return jnp.where(exists, row, jnp.zeros_like(row))


def borders():
    mine = lax.axis_index("rows")
    return lax.rem(mine, 2) == 0, mine > 0, mine < lax.axis_size("rows") - 1


def tables_kernel(band, across, slots, row_hbm, col_hbm, feat_hbm, state_hbm,
                  table_ref, near_ref, far_ref, near_edge, far_edge, pool_ref, row_ref, col_ref, sem):
    frames, blocks = row_ref.shape
    rows = feat_hbm.shape[1]
    mine = lax.axis_index("rows")
    total = band * lax.axis_size("rows")
    even = lax.rem(mine, 2) == 0
    moves = [
        pltpu.make_async_copy(row_hbm, row_ref, sem.at[0]),
        pltpu.make_async_copy(col_hbm, col_ref, sem.at[1]),
    ]
    near_rows = pl.ds(jnp.where(even, rows - HALO, 0), HALO)
    far_rows = pl.ds(jnp.where(even, 0, rows - HALO), HALO)
    edges = [
        pltpu.make_async_copy(feat_hbm.at[0, near_rows], near_edge, sem.at[2]),
        pltpu.make_async_copy(feat_hbm.at[0, far_rows], far_edge, sem.at[3]),
    ]
    for copy in moves + edges:
        copy.start()
    for q in range(band):
        for r in range(BLK):
            pltpu.make_async_copy(
                state_hbm.at[q, r], pool_ref.at[pl.ds(q * across, across), r], sem.at[4]
            ).start()
    for copy in moves:
        copy.wait()
    block = lax.broadcasted_iota(jnp.int32, (frames, blocks), 1)
    source = jnp.clip(block // across + row_ref[...], -mine * band, total - 1 - mine * band)
    column = jnp.clip(block % across + col_ref[...], 0, across - 1)
    above = source < 0
    below = source >= band
    local = source * across + column + jnp.where(above, blocks, jnp.where(below, -blocks, 0))
    earlier = lax.broadcasted_iota(jnp.int32, (blocks, blocks), 0) < lax.broadcasted_iota(
        jnp.int32, (blocks, blocks), 1
    )
    earlier = jnp.where(earlier, 1.0, 0.0).astype(BF16)

    def rank(mask):
        ones = jnp.where(mask, 1.0, 0.0).astype(BF16)
        return jnp.dot(ones, earlier, preferred_element_type=F32).astype(jnp.int32)

    rank_above = rank(above)
    rank_below = rank(below)
    near_base = blocks
    far_base = blocks + slots
    above_base = jnp.where(even, far_base, near_base)
    below_base = jnp.where(even, near_base, far_base)
    table = jnp.where(above, above_base + rank_above, local)
    table_ref[...] = jnp.where(below, below_base + rank_below, table)
    near_rank = jnp.where(even, jnp.where(below, rank_below, -1), jnp.where(above, rank_above, -1))
    far_rank = jnp.where(even, jnp.where(above, rank_above, -1), jnp.where(below, rank_below, -1))
    length = near_ref.shape[1]
    slot = lax.broadcasted_iota(jnp.int32, (length, blocks), 0)
    for frame in range(frames):
        ids = local[frame:frame + 1].astype(F32).astype(BF16)
        for ranks, out in ((near_rank, near_ref), (far_rank, far_ref)):
            chosen = jnp.where(ranks[frame:frame + 1] == slot, 1.0, 0.0).astype(BF16)
            got = lax.dot_general(ids, chosen, (((1,), (1,)), ((), ())), preferred_element_type=F32)
            out[frame:frame + 1] = got.astype(jnp.int32)
    for copy in edges:
        copy.wait()
    own = pool_ref.at[pl.ds(0, blocks)]
    pltpu.make_async_copy(own, own, sem.at[4]).wait()


def weights_kernel(merging_hbm, first_hbm, second_hbm, _,
                   feat_out, warp_out, first_out, second_out, merging_ref, first_ref, second_ref, sem):
    loads = [
        pltpu.make_async_copy(merging_hbm, merging_ref, sem.at[0]),
        pltpu.make_async_copy(first_hbm, first_ref, sem.at[1]),
        pltpu.make_async_copy(second_hbm, second_ref, sem.at[2]),
    ]
    for load in loads:
        load.start()
    chans = first_ref.shape[2]
    depth = 3 * chans
    for source, start, out, load in (
        (merging_ref, 0, feat_out, loads[0]),
        (merging_ref, chans, warp_out, None),
        (first_ref, 0, first_out, loads[1]),
        (second_ref, 0, second_out, loads[2]),
    ):
        if load is not None:
            load.wait()
        width = source.shape[3]
        zero = jnp.zeros((chans, width), BF16)
        for a in range(4):
            for e in range(3):
                top = a * depth + e * chans
                for half in range(2):
                    tap = a - half
                    if 0 <= tap < 3:
                        value = source[tap, e, start:start + chans, :]
                    else:
                        value = zero
                    out[top:top + chans, half * width:(half + 1) * width] = value


def pack(pool_ref, near_list, far_list, frame, near_out, far_out):
    for slot in range(near_out.shape[0]):
        near_out[slot] = pool_ref[near_list[frame, slot]]
        far_out[slot] = pool_ref[far_list[frame, slot]]


def pack_kernel(frame, pool_ref, near_list, far_list, near_out, far_out):
    pack(pool_ref, near_list, far_list, frame, near_out, far_out)


def shifter(pad_ref):
    slots, length, chans = pad_ref.shape
    cols = length - 2 * BLK
    edge = jnp.zeros((BLK, chans), F32)
    for slot in range(slots):
        pad_ref[slot, 0:BLK] = edge
        pad_ref[slot, BLK + cols:length] = edge
    turn = [0]

    def spread(out_ref, pair, half, value):
        slot = turn[0] % slots
        turn[0] += 1
        pad_ref[slot, BLK:BLK + cols] = value
        left = pad_ref[slot, BLK - 1:BLK - 1 + cols]
        right = pad_ref[slot, BLK + 1:BLK + 1 + cols]
        for e, part in enumerate((left, value, right)):
            out_ref[pair, half, :, e * chans:(e + 1) * chans] = part.astype(BF16)

    return spread


def pair_dot(x_ref, w_ref, pair, pairs):
    cols, depth = x_ref.shape[2:]
    parts = [
        x_ref[pair + a // 2:pair + a // 2 + pairs, a % 2].reshape(pairs * cols, depth)
        for a in range(4)
    ]
    return jnp.dot(jnp.concatenate(parts, axis=1), w_ref[...], preferred_element_type=F32)


def chunks(first, end, size):
    total = end - first
    count = -(-total // size)
    bounds = [first + total * n // count for n in range(count + 1)]
    return [(a, b - a) for a, b in zip(bounds, bounds[1:])]


def features_kernel(frame, passed, feat_hbm, near_ref, far_ref, w_ref, *refs):
    feat_ref, x_ref, pad_ref, sem, edge_sem = refs[-5:]
    outs = refs[min(frame, 2):-5]
    out_ref, edges = outs[0], outs[1:1 + passed]
    rows, across, _, chans = feat_ref.shape
    cols = across * BLK
    even, has_above, has_below = borders()
    size = rows // sem.shape[0]
    spread = shifter(pad_ref)
    loads = []
    for n in range(sem.shape[0]):
        part = pl.ds(n * size, size)
        loads.append(pltpu.make_async_copy(feat_hbm.at[frame, part], feat_ref.at[part], sem.at[n]))
        loads[-1].start()
    starts = (jnp.where(even, rows - HALO, 0), jnp.where(even, 0, rows - HALO))
    for n, edge in enumerate(edges):
        part = pl.ds(starts[n], HALO)
        loads.append(pltpu.make_async_copy(feat_hbm.at[frame + 1, part], edge, edge_sem.at[n]))
        loads[-1].start()
    if frame:
        loads.append(pltpu.make_async_copy(refs[0], outs[-1].at[frame - 1], edge_sem.at[2]))
        loads[-1].start()
    for row in range(-HALO, rows + HALO):
        if row < 0:
            n = row + near_ref.shape[0]
            value = halo_row(near_ref[n], far_ref[n], even, has_above, True)
        elif row >= rows:
            n = row - rows + near_ref.shape[0] - HALO
            value = halo_row(near_ref[n], far_ref[n], even, has_below, False)
        else:
            if row % size == 0:
                loads[row // size].wait()
            value = feat_ref[row]
        value = value.astype(F32).reshape(cols, chans)
        spread(x_ref, (row + HALO) // 2, (row + HALO) % 2, value)
    for pair, pairs in chunks(0, rows // 2 + 2, STEP):
        out_ref[pair:pair + pairs] = pair_dot(x_ref, w_ref, pair, pairs).reshape(
            pairs, cols, out_ref.shape[2]
        )
    for load in loads[sem.shape[0]:]:
        load.wait()


def assemble_kernel(frame, table_vmem, pool_ref, near_ref, far_ref, _, *refs):
    warped_out, near_edge, far_edge, all_ref, table_ref, table_sem = refs[-6:]
    table_copy = pltpu.make_async_copy(table_vmem, table_ref, table_sem)
    table_copy.start()
    rows, across = warped_out.shape[:2]
    blocks = table_vmem.shape[1]
    slots = near_ref.shape[0]
    odd = lax.rem(lax.axis_index("rows"), 2)
    near_rows = pl.ds(jnp.where(odd == 0, rows - HALO, 0), HALO)
    far_rows = pl.ds(jnp.where(odd == 0, 0, rows - HALO), HALO)
    for edge, feat_edge in zip((near_edge, far_edge), refs[:-6]):
        edge[HALO:2 * HALO] = feat_edge[...]
    all_ref[blocks:blocks + slots] = near_ref[...]
    all_ref[blocks + slots:blocks + 2 * slots] = far_ref[...]
    table_copy.wait()
    for block in range(blocks):
        q, p = divmod(block, across)
        warped_out[q * BLK:(q + 1) * BLK, p] = all_ref[table_ref[frame, block]]
    near_edge[0:HALO] = warped_out[near_rows]
    far_edge[0:HALO] = warped_out[far_rows]


def split_rows(value, pairs, cols, chans):
    for n in range(pairs):
        for half in range(2):
            yield n, half, value[n * cols:(n + 1) * cols, half * chans:(half + 1) * chans]


def finish(state_ref, pool_ref, centre, value, row, across, chans):
    done = (centre.astype(F32) + value).reshape(across, BLK, chans).astype(BF16)
    state_ref[row] = done
    if pool_ref is not None:
        q, r = divmod(row, BLK)
        pool_ref[q * across:(q + 1) * across, r] = done


def inner_kernel(last, part_ref, warped_ref, w1_ref, w2_ref, w3_ref, state_ref, *refs):
    pool_ref = None if last else refs[0]
    m_edge, d_edge, x_ref, m_ref, d_ref, pad_ref = refs[-6:]
    spread = shifter(pad_ref)
    rows, across, _, chans = warped_ref.shape
    cols = across * BLK
    half_rows = rows // 2
    for row in range(rows):
        value = warped_ref[row].astype(F32).reshape(cols, chans)
        spread(x_ref, (row + HALO) // 2, (row + HALO) % 2, value)
    for pair, pairs in chunks(2, half_rows, STEP):
        raw = part_ref[pair:pair + pairs].reshape(pairs * cols, 2 * chans)
        raw = raw + pair_dot(x_ref, w1_ref, pair, pairs)
        value = jnp.maximum(raw, 0.1 * raw)
        for n, half, one in split_rows(value, pairs, cols, chans):
            spread(m_ref, pair + n, half, one)
    m_edge[0] = m_ref[2]
    m_edge[1] = m_ref[half_rows - 1]
    for pair, pairs in chunks(2, half_rows - 1, STEP):
        value = jnp.maximum(pair_dot(m_ref, w2_ref, pair, pairs), 0.0)
        for n, half, one in split_rows(value, pairs, cols, chans):
            spread(d_ref, pair + n, half, one)
    d_edge[0] = d_ref[2]
    d_edge[1] = d_ref[half_rows - 2]
    for pair, pairs in chunks(2, half_rows - 2, STEP):
        value = pair_dot(d_ref, w3_ref, pair, pairs)
        for n, half, one in split_rows(value, pairs, cols, chans):
            centre = m_ref[pair + n + 1, half, :, chans:2 * chans]
            finish(state_ref, pool_ref, centre, one, 2 * (pair + n) + half, across, chans)


def border_kernel(frame, last, part_ref, warped_ref, near_ref, far_ref, w1_ref, w2_ref, w3_ref,
                  m_edge, d_edge, *refs):
    if last:
        state_in, _, out_ref, x_ref, m_ref, d_ref, pad_ref, sem, state_ref = refs
        pool_ref = None
        inner = pl.ds(4, warped_ref.shape[0] - 8)
        copies = [pltpu.make_async_copy(state_in.at[inner], out_ref.at[frame, inner], sem.at[2])]
        copies[0].start()
    else:
        _, _, near_vmem, far_vmem, state_ref, pool_ref, near_out, far_out = refs[:8]
        x_ref, m_ref, d_ref, pad_ref, sem, near_list, far_list = refs[8:]
        lists = [
            pltpu.make_async_copy(near_vmem, near_list, sem.at[2]),
            pltpu.make_async_copy(far_vmem, far_list, sem.at[3]),
        ]
        for copy in lists:
            copy.start()
    spread = shifter(pad_ref)
    rows, across, _, chans = warped_ref.shape
    cols = across * BLK
    even, has_above, has_below = borders()
    depth = 3 * chans

    def edge_dot(ref, side, w_ref):
        parts = [ref[side, a // 2:a // 2 + 2, a % 2].reshape(2 * cols, depth) for a in range(4)]
        return jnp.dot(jnp.concatenate(parts, axis=1), w_ref[...], preferred_element_type=F32)

    def flat(value):
        return value.astype(F32).reshape(cols, chans)

    for n in range(HALO):
        above = halo_row(near_ref[n], far_ref[n], even, has_above, True)
        below = halo_row(near_ref[n], far_ref[n], even, has_below, False)
        spread(x_ref.at[0], n // 2, n % 2, flat(above))
        spread(x_ref.at[0], (n + 3) // 2, (n + 3) % 2, flat(warped_ref[n]))
        spread(x_ref.at[1], n // 2, n % 2, flat(warped_ref[rows - HALO + n]))
        spread(x_ref.at[1], (n + 3) // 2, (n + 3) % 2, flat(below))
    half_rows = rows // 2

    def masked(value, row):
        if row < 0:
            return jnp.where(has_above, value, 0.0)
        return jnp.where(has_below, value, 0.0) if row >= rows else value

    m_ref[0, 2] = m_edge[0]
    m_ref[1, 0] = m_edge[1]
    d_ref[0, 2] = d_edge[0]
    d_ref[1, 0] = d_edge[1]
    for side in range(2):
        first = side * half_rows
        raw = part_ref[first:first + 2].reshape(2 * cols, 2 * chans) + edge_dot(x_ref, side, w1_ref)
        value = jnp.maximum(raw, 0.1 * raw)
        for n, half, one in split_rows(value, 2, cols, chans):
            one = masked(one, 2 * (first + n) + half - 2)
            spread(m_ref.at[side], n + side, half, one)
    for side in range(2):
        first = side * (half_rows - 1)
        value = jnp.maximum(edge_dot(m_ref, side, w2_ref), 0.0)
        for n, half, one in split_rows(value, 2, cols, chans):
            one = masked(one, 2 * (first + n) + half - 1)
            spread(d_ref.at[side], n + side, half, one)
    for side in range(2):
        first = side * (half_rows - 2)
        value = edge_dot(d_ref, side, w3_ref)
        for n, half, one in split_rows(value, 2, cols, chans):
            centre = m_ref[side, n + 1 - side, half, :, chans:2 * chans]
            finish(state_ref, pool_ref, centre, one, 2 * (first + n) + half, across, chans)
        if last:
            part = pl.ds(side * (rows - 4), 4)
            copies.append(pltpu.make_async_copy(state_ref.at[part], out_ref.at[frame, part], sem.at[side]))
            copies[-1].start()
    if last:
        for copy in copies:
            copy.wait()
    else:
        for copy in lists:
            copy.wait()
        pack(pool_ref, near_list, far_list, frame + 1, near_out, far_out)


def on_device(state_start, features, row_moves, col_moves, merging_weight, first_weight, second_weight):
    rows, cols, chans = state_start.shape
    frames = features.shape[0]
    band = rows // BLK
    across = cols // BLK
    blocks = band * across
    slots = blocks // 2
    list_len = slots + 8
    state = state_start.reshape(band, BLK, across, BLK, chans)
    feats = features.reshape(frames, rows, across, BLK, chans)
    block_shape = (BLK, BLK, chans)
    edge_shape = (HALO, across, BLK, chans)
    pool_shape = on_chip((blocks + 2 * slots,) + block_shape)
    message = on_chip((slots,) + block_shape)

    table, near_list, far_list, near_feat, far_feat, pool = pl.pallas_call(
        functools.partial(tables_kernel, band, across, slots),
        out_shape=[
            on_chip((frames, blocks), jnp.int32),
            on_chip((frames, list_len), jnp.int32),
            on_chip((frames, list_len), jnp.int32),
            on_chip(edge_shape),
            on_chip(edge_shape),
            pool_shape,
        ],
        in_specs=[ANY] * 4,
        out_specs=[VMEM] * 6,
        scratch_shapes=[
            pltpu.VMEM((frames, blocks), jnp.int32),
            pltpu.VMEM((frames, blocks), jnp.int32),
            pltpu.SemaphoreType.DMA((5,)),
        ],
        compiler_params=room(4),
        name="tables",
    )(*map(in_hbm, (row_moves, col_moves, feats, state)))
    near_list, far_list = swap_both(near_list, far_list)
    near_feat, far_feat = swap_both(near_feat, far_feat)

    near_msg, far_msg = pl.pallas_call(
        functools.partial(pack_kernel, 0),
        out_shape=[message, message],
        in_specs=[VMEM, SMEM, SMEM],
        out_specs=[VMEM] * 2,
        compiler_params=room(4),
        name="pack",
    )(resident(pool), near_list, far_list)

    pair_shape = on_chip((4 * 3 * chans, 2 * chans))
    w_feat, w_warp, w_first, w_second = pl.pallas_call(
        weights_kernel,
        out_shape=[pair_shape] * 4,
        in_specs=[ANY] * 4,
        out_specs=[VMEM] * 4,
        scratch_shapes=[
            pltpu.VMEM(merging_weight.shape, BF16),
            pltpu.VMEM(first_weight.shape, BF16),
            pltpu.VMEM(second_weight.shape, BF16),
            pltpu.SemaphoreType.DMA((3,)),
        ],
        compiler_params=room(4),
        name="weights",
    )(*map(in_hbm, (merging_weight, first_weight, second_weight)), near_msg)

    pad_rows = pltpu.VMEM((24, cols + 2 * BLK, chans), F32)

    def wide(extra):
        return pltpu.VMEM((rows // 2 + extra, 2, cols, 3 * chans), BF16)

    out_shape = shape_of((frames, rows, across, BLK, chans))

    def features_part(frame, near_feat, far_feat, before, out):
        passed = 0 if frame == frames - 1 else 2
        done = ([resident(before)] if frame else []) + ([out] if frame > 1 else [])
        return pl.pallas_call(
            functools.partial(features_kernel, frame, passed),
            out_shape=[on_chip((rows // 2 + 2, cols, 2 * chans), F32)]
            + [on_chip(edge_shape)] * passed
            + [out_shape] * (frame > 0),
            in_specs=[ANY] + [VMEM] * 3 + [VMEM] * (frame > 0) + [ANY] * (frame > 1),
            out_specs=[VMEM] * (1 + passed) + [ANY] * (frame > 0),
            input_output_aliases={5: 1 + passed} if frame > 1 else {},
            scratch_shapes=[
                pltpu.VMEM((rows, across, BLK, chans), BF16),
                wide(3),
                pad_rows,
                pltpu.SemaphoreType.DMA((4,)),
                pltpu.SemaphoreType.DMA((3,)),
            ],
            compiler_params=room(16),
            name="features",
        )(in_hbm(feats), resident(near_feat), resident(far_feat), resident(w_feat), *done)

    out = state_now = None
    state_shape = on_chip((rows, across, BLK, chans))
    edge_pairs = on_chip((2, 2, cols, 3 * chans))
    for frame in range(frames):
        last = frame == frames - 1
        near_got, far_got = swap_both(near_msg, far_msg)
        part, *next_edges = features_part(frame, near_feat, far_feat, state_now, out)
        if frame:
            out = next_edges.pop()
        sent_edge = on_chip(((1 if last else 2) * HALO,) + edge_shape[1:])
        warped, near_edge, far_edge, _ = pl.pallas_call(
            functools.partial(assemble_kernel, frame),
            out_shape=[on_chip((rows, across, BLK, chans)), sent_edge, sent_edge, pool_shape],
            in_specs=[VMEM] * 4 + [ANY] + [VMEM] * len(next_edges),
            out_specs=[VMEM] * 4,
            input_output_aliases={1: 3},
            scratch_shapes=[
                pltpu.SMEM((frames, blocks), jnp.int32),
                pltpu.SemaphoreType.DMA,
            ],
            compiler_params=room(8),
            name="assemble",
        )(resident(table), resident(pool), resident(near_got), resident(far_got), part, *map(resident, next_edges))
        near_halo, far_halo = swap_both(near_edge, far_edge)
        near_feat, far_feat = near_halo, far_halo
        args = tuple(map(resident, (part, warped, w_warp, w_first, w_second)))
        state_now, *results = pl.pallas_call(
            functools.partial(inner_kernel, last),
            out_shape=[state_shape] + [pool_shape] * (not last) + [edge_pairs] * 2,
            in_specs=[VMEM] * 5,
            out_specs=[VMEM] * (3 + (not last)),
            scratch_shapes=[wide(3), wide(2), wide(1), pad_rows],
            compiler_params=room(24),
            name="inner",
        )(*args)
        m_edge, d_edge = results[-2:]
        args = tuple(map(resident, (
            part, warped, near_halo, far_halo, w_warp, w_first, w_second, m_edge, d_edge
        )))
        scratch = [pltpu.VMEM((2, 3, 2, cols, 3 * chans), BF16) for _ in range(3)] + [
            pad_rows,
            pltpu.SemaphoreType.DMA((4,)),
        ]
        if last:
            scratch.append(pltpu.VMEM((rows, across, BLK, chans), BF16))
        else:
            scratch += [pltpu.SMEM((frames, list_len), jnp.int32)] * 2
        kernel = functools.partial(border_kernel, frame, last)
        if last:
            out = pl.pallas_call(
                kernel,
                out_shape=out_shape,
                in_specs=[VMEM] * 10 + [ANY],
                out_specs=ANY,
                input_output_aliases={10: 0},
                scratch_shapes=scratch,
                compiler_params=room(12),
                name="border",
            )(*args, resident(state_now), out)
        else:
            state_now, pool, near_msg, far_msg = pl.pallas_call(
                kernel,
                out_shape=[state_shape, pool_shape, message, message],
                in_specs=[VMEM] * 13,
                out_specs=[VMEM] * 4,
                input_output_aliases={9: 0, 10: 1},
                scratch_shapes=scratch,
                compiler_params=room(12),
                name="border",
            )(*args, *map(resident, (state_now, results[0], near_list, far_list)))
    return out.reshape(frames, rows, cols, chans)


def solution(mesh):
    in_specs = (
        P(("clips", "rows"), None, None),
        P(None, ("clips", "rows"), None, None),
        P(None, ("clips", "rows")),
        P(None, ("clips", "rows")),
        P(),
        P(),
        P(),
    )
    out_specs = P(None, ("clips", "rows"), None, None)
    return jax.shard_map(
        on_device, mesh=mesh, in_specs=in_specs, out_specs=out_specs, check_vma=False
    )
```
